512 devices in a mesh: surf: 64 (over x, y, z_lo), field: 8 (over z_hi, core).
Axes of the slice: x: 4, y: 4, z: 16 (z_hi: 4, z_lo: 4; z = z_hi * 4 + z_lo), core: 2. Of those that a mesh axis runs over, the one named last changes fastest.
Arguments:
- forces: bfloat16 [4, 2, 512, 128], P(None, None, 'surf'), may hold values from -6 to 6
- response: bfloat16 [4, 2, 65536, 512], P(None, None, ('surf', 'field'))
- panel_plane: float32 [2, 65536], P(None, 'surf'), may hold values from -1 to 1
- panel_area: float32 [65536], P('surf'), may hold values from 0.002 to 0.008
- field_points: float32 [3, 4096], P(None, 'field'), may hold values from -1.1 to 1.1, as said below
- wavenumber: float32 [4], replicated, may hold values from 2 to 8
Outputs:
- pressure: bfloat16 [4096, 4, 2, 128], P(('field', 'surf'))
- efficiency: float32 [4, 128], replicated
The draws below stay inside these ranges and needn't reach their ends.
Inputs may be any that keep to these rules, and one draw needn't show every extreme that they name: `field_points`: rows are x, y and height; heights lie between 0.02 and 0.7.
All inputs are finite; a program needn't handle non-finite values.
Results may differ from the reference program's by a relative error of at most 0.0058.
Values may be sent and summed in bfloat16 or wider, within the bound.
No kernel may reach another device: no remote copies, remote signals or barrier semaphores. Data moves between devices by JAX's collectives and lax.ppermute only.
A program may use at most 64 MiB of HBM per device.

```python
import math
import jax
import jax.numpy as jnp
from jax import lax

LINES = 4
CHANNELS = 512
CASES = 128
PANELS = 65536
POINTS = 4096


def draw_response(key, part):
    shape = (LINES, 2, PANELS, CHANNELS)
    values = jnp.clip(jax.random.normal(key, shape, jnp.float32), -6.0, 6.0)
    growth = math.log(3.0)
    position = jnp.arange(PANELS, dtype=jnp.float32) / PANELS
    scaling = jnp.exp(growth * position)[None, None, :, None] / math.sqrt(CHANNELS)
    return (values * scaling).astype(jnp.bfloat16)


def draw_field_points(key, part):
    key_plane = jax.random.fold_in(key, 11)
    key_height = jax.random.fold_in(key, 12)
    plane = jax.random.uniform(key_plane, (2, POINTS), jnp.float32, -1.0, 1.0)
    top_height = 0.6
    descent = math.log(12.0)
    factor = jax.random.uniform(key_height, (1, POINTS), jnp.float32, math.log(0.5), 0.0)
    position = jnp.arange(POINTS, dtype=jnp.float32)[None, :] / POINTS
    height = top_height * jnp.exp(factor - descent * position)
    return jnp.concatenate([plane, height], axis=0).astype(jnp.float32)


def shard_levels(key, dims, split, least, largest):
    factor_of = 1.0
    for dim, shards_of in split:
        heights = jax.random.uniform(jax.random.fold_in(jax.random.fold_in(key, 6), dim), (shards_of,), jnp.float32, least / len(split), largest / len(split))
        factor_of = factor_of * jnp.repeat(jnp.exp(heights), dims[dim] // shards_of).reshape((-1,) + (1,) * (len(dims) - 1 - dim))
    return factor_of


def scatter_about(own_key, extent, scale, most, split=(), kind=jnp.bfloat16):
    array = scale * jax.random.normal(own_key, extent, jnp.float32)
    if split:
        array = array * shard_levels(own_key, extent, split, -0.22, 0.18)
    return jnp.clip(array, -most, most).astype(kind)


def setup_inputs(seed: int = 0) -> dict:
    splits = jax.random.split(jax.random.key(seed), 7)
    forces = scatter_about(splits[0], (LINES, 2, CHANNELS, CASES), 1.0, 6.0, ((2, 64),))
    response = draw_response(jax.random.fold_in(splits[6], 71), 0)
    panel_plane = jnp.clip(jax.random.uniform(splits[2], (2, PANELS), jnp.float32, -1.0, 1.0) * shard_levels(splits[2], (2, PANELS), ((1, 64),), -0.4, 0.0), -1.0, 1.0)
    panel_area = jnp.clip(jnp.exp(math.log(0.008) - 1.3862944 * jax.random.uniform(splits[3], (PANELS,), jnp.float32) ** shard_levels(splits[3], (PANELS,), ((0, 64),), -0.2, 0.2)), 0.002, 0.008)
    field_points = draw_field_points(jax.random.fold_in(splits[6], 71), 0)
    wavenumber = jnp.clip(jnp.exp(jax.random.uniform(splits[5], (LINES,), jnp.float32, math.log(2.0), math.log(8.0))), 2.0, 8.0)
    return dict(forces=forces, response=response, panel_plane=panel_plane, panel_area=panel_area, field_points=field_points, wavenumber=wavenumber)


def complex_matrix(real_part, imag_part):
    upper = jnp.concatenate([real_part, imag_part], axis=-1)
    lower = jnp.concatenate([-imag_part, real_part], axis=-1)
    return jnp.concatenate([upper, lower], axis=0)

def plane_distance(points, panel_plane):
    offset_x = points[0][:, None] - panel_plane[0][None, :]
    offset_y = points[1][:, None] - panel_plane[1][None, :]
    height = points[2][:, None]
    return jnp.sqrt(offset_x * offset_x + offset_y * offset_y + height * height)

def kernel_tiles(distance, panel_area, wave):
    phase = wave * distance
    sine_part = panel_area[None, :] * jnp.sin(phase) / distance
    cosine_part = panel_area[None, :] * jnp.cos(phase) / distance
    return jnp.concatenate([sine_part, cosine_part], axis=1).astype(jnp.bfloat16)

def reference(forces, response, panel_plane, panel_area, field_points, wavenumber):
    velocity_list = []
    for line in range(LINES):
        operand = jnp.concatenate([response[line, 0], response[line, 1]], axis=1)
        driving = complex_matrix(forces[line, 0], forces[line, 1])
        velocity_list.append(jnp.dot(operand, driving, preferred_element_type=jnp.float32).astype(jnp.bfloat16))
    velocity = jnp.stack(velocity_list)
    squares = lax.optimization_barrier(jnp.sum(jnp.square(velocity.astype(jnp.float32)), axis=1))
    energy = squares[:, :CASES] + squares[:, CASES:]
    stacked = [complex_matrix(velocity[line, :, :CASES], velocity[line, :, CASES:]) for line in range(LINES)]
    block = 128 if POINTS % 128 == 0 else POINTS
    count = POINTS // block
    blocks = field_points.reshape(3, count, block).transpose(1, 0, 2)

    def one_block(points):
        distance = plane_distance(points, panel_plane)
        results = []
        for line in range(LINES):
            tiles = kernel_tiles(distance, panel_area, wavenumber[line])
            summed = jnp.dot(tiles, stacked[line], preferred_element_type=jnp.float32)
            results.append(wavenumber[line] / (2.0 * math.pi) * summed)
        return jnp.stack(results, axis=1).astype(jnp.bfloat16)
    pressure = lax.map(one_block, blocks).reshape(POINTS, LINES, 2, CASES)
    power = lax.optimization_barrier(jnp.sum(jnp.square(pressure.astype(jnp.float32)), axis=(0, 2)))
    efficiency = power / POINTS / (energy / PANELS + 1e-06)
    return (pressure, efficiency)
```

```python
import math

import jax
import jax.numpy as jnp
import numpy as np
from jax import lax
from jax.sharding import Mesh, PartitionSpec as P

SURF = ("x", "y", "zl")
FIELD = ("zh", "c")
DEPTH = ("zh", "zl")
SWAP = [(0, 1), (1, 0)]


def complex_matrix(real_part, imag_part):
    upper = jnp.concatenate([real_part, imag_part], axis=-1)
    lower = jnp.concatenate([-imag_part, real_part], axis=-1)
    return jnp.concatenate([upper, lower], axis=0)


def plane_distance(points, panel_plane):
    offset_x = points[0][:, None] - panel_plane[0][None, :]
    offset_y = points[1][:, None] - panel_plane[1][None, :]
    height = points[2][:, None]
    return jnp.sqrt(offset_x * offset_x + offset_y * offset_y + height * height)


def kernel_tiles(distance, panel_area, wave):
    phase = wave * distance
    sine_part = panel_area[None, :] * jnp.sin(phase) / distance
    cosine_part = panel_area[None, :] * jnp.cos(phase) / distance
    return jnp.concatenate([sine_part, cosine_part], axis=1).astype(jnp.bfloat16)


def exchange(array, axes):
    return lax.all_to_all(array, axes, 0, 0, tiled=True)


def gather(array, axes):
    size = lax.axis_size(axes)
    return exchange(jnp.broadcast_to(array[None], (size,) + array.shape), axes)


def ring_gather(array, axis):
    size = lax.axis_size(axis)
    me = lax.axis_index(axis)
    parts = [array]
    for step in range(1, size):
        parts.append(lax.ppermute(array, axis, [(i, (i - step) % size) for i in range(size)]))
    twice = jnp.stack(parts + parts)
    return lax.dynamic_slice_in_dim(twice, (size - me) % size, size, 0)


def shards(forces, response, panel_plane, panel_area, field_points, wavenumber):
    lines, _, channels, cases = forces.shape
    own = response.shape[2]
    x_size, y_size = lax.axis_size("x"), lax.axis_size("y")
    depth_size = lax.axis_size(DEPTH)
    core = lax.axis_index("c")
    rows = field_points.shape[1] // lax.axis_size(SURF)
    share = rows * y_size * lax.axis_size("zl")

    my_points = lax.dynamic_slice_in_dim(field_points, lax.axis_index("x") * share, share, 1)
    all_points = ring_gather(my_points, "zh")
    points = all_points.reshape(-1, 3, y_size, share // y_size).transpose(1, 2, 0, 3).reshape(3, -1)

    panels = jnp.concatenate([panel_plane, panel_area[None]], axis=0)
    my_panels = lax.dynamic_slice_in_dim(panels, lax.axis_index("zh") * 2 * own, 2 * own, 1)
    panels = gather(my_panels, "x")
    panels = panels.reshape(x_size, 3, 2, own).transpose(1, 2, 0, 3)
    panels = jnp.where(core == 0, panels, panels[:, ::-1]).reshape(3, -1)

    part = jnp.where(core == 0, forces[:, 0], forces[:, 1])
    part = gather(part, SURF)
    part = part.transpose(1, 0, 2, 3).reshape(lines, -1, cases)
    other = lax.ppermute(part, "c", SWAP)
    real_part = jnp.where(core == 0, part, other)
    imag_part = jnp.where(core == 0, other, part)

    velocity_list = []
    for line in range(lines):
        operand = jnp.concatenate([response[line, 0], response[line, 1]], axis=1)
        driving = complex_matrix(real_part[line], imag_part[line])
        velocity_list.append(
            jnp.dot(operand, driving, preferred_element_type=jnp.float32).astype(jnp.bfloat16)
        )
    velocity = jnp.stack(velocity_list)
    squares = jnp.sum(jnp.square(velocity.astype(jnp.float32)), axis=1)
    energy_part = squares[:, :cases] + squares[:, cases:]

    near = gather(velocity, "x")
    shared = jnp.stack([near, lax.ppermute(near, "c", SWAP)])
    shared = shared.transpose(2, 0, 1, 3, 4).reshape(lines, -1, 2 * cases)

    distance = plane_distance(points, panels)
    partial = []
    for line in range(lines):
        tiles = kernel_tiles(distance, panels[2], wavenumber[line])
        stacked = complex_matrix(shared[line, :, :cases], shared[line, :, cases:])
        summed = jnp.dot(tiles, stacked, preferred_element_type=jnp.float32)
        partial.append(summed.astype(jnp.bfloat16).reshape(y_size, -1, 2 * cases))
    partial = jnp.stack(partial, axis=1)

    beside = exchange(partial, "y")
    level = jnp.sum(beside.astype(jnp.float32), axis=0).astype(jnp.bfloat16)
    level = level.reshape(lines, depth_size, rows, 2 * cases).transpose(1, 0, 2, 3)
    column = exchange(level, DEPTH)
    total = jnp.sum(column.astype(jnp.float32), axis=0)
    total = total * (wavenumber / (2.0 * math.pi))[:, None, None]
    pressure = total.astype(jnp.bfloat16)
    power = jnp.sum(jnp.square(pressure.astype(jnp.float32)), axis=1)
    power_part = power[:, :cases] + power[:, cases:]

    sums = jnp.concatenate([energy_part, power_part], axis=0)
    sums = jnp.sum(gather(sums, ("x", "y")), axis=0)
    sums = jnp.sum(gather(sums, DEPTH + ("c",)), axis=0)
    point_total = field_points.shape[1] * lax.axis_size(FIELD)
    panel_total = own * lax.axis_size(SURF + FIELD)
    efficiency = sums[lines:] / point_total / (sums[:lines] / panel_total + 1e-06)
    pressure = pressure.transpose(1, 0, 2).reshape(rows, lines, 2, cases)
    return (pressure, efficiency)


def solution(mesh):
    grid = Mesh(np.asarray(mesh.devices).reshape(4, 4, 4, 4, 2), SURF + FIELD)
    return jax.shard_map(
        shards,
        mesh=grid,
        in_specs=(
            P(None, None, SURF, None),
            P(None, None, SURF + FIELD, None),
            P(None, SURF),
            P(SURF),
            P(None, FIELD),
            P(),
        ),
        out_specs=(P(FIELD + SURF, None, None, None), P()),
        check_vma=False,
    )
```

```python
import functools
import math

import jax
import jax.numpy as jnp
import numpy as np
from jax import lax
from jax.experimental import pallas as pl
from jax.experimental.pallas import tpu as pltpu
from jax.sharding import Mesh, PartitionSpec as P

SURF = ("x", "y", "zl")
FIELD = ("zh", "c")
DEPTH = ("zh", "zl")
LEVEL = ("x", "y", "c")
SWAP = [(0, 1), (1, 0)]
LANES = 128
STRIP = 32
THIRDS = 16
BF16 = jnp.bfloat16
F32 = jnp.float32


def fitted(function, count):
    top = 0.0625
    nodes = 0.5 * top * (1.0 - np.cos(np.pi * (np.arange(count) + 0.5) / count))
    powers = np.vander(nodes, count, increasing=True)
    return [float(value) for value in np.linalg.solve(powers, function(np.sqrt(nodes)))]


SINE = fitted(lambda b: np.sin(2.0 * np.pi * b) / b, 5)
COSINE = fitted(lambda b: np.cos(2.0 * np.pi * b), 5)


def polynomial(coefficients, u):
    total = u * coefficients[-1] + coefficients[-2]
    for value in coefficients[-3::-1]:
        total = total * u + value
    return total


def tile_kernel(place, wave, own, first, second, third, mine, other, out, px, py, pz):
    lines = out.shape[1]
    depth = 4

    @pl.when((pl.program_id(0) == 0) & (pl.program_id(1) == 0))
    def _():
        for back, block in enumerate((own, first, second, third)):
            slot = lax.rem(place[0] + depth - back, depth)
            for coordinate, target in enumerate((px, py, pz)):
                row = block[coordinate : coordinate + 1, :]
                if coordinate == 2:
                    row = row * row
                column = jnp.broadcast_to(row, (LANES, LANES)).T
                for part in range(4):
                    start = pl.multiple_of(part * LANES + slot * STRIP, STRIP)
                    target[pl.ds(start, STRIP), :] = column[part * STRIP : (part + 1) * STRIP, :]

    thirds = jnp.where(pl.program_id(0) == 0, mine[0].astype(F32), other[0].astype(F32))
    across = thirds[0:1] + thirds[1:2] + thirds[2:3]
    along = thirds[3:4] + thirds[4:5] + thirds[5:6]
    area = thirds[6:7] + thirds[7:8] + thirds[8:9]
    turns = [wave[line] * (0.5 / math.pi) for line in range(lines)]

    def strip(index, carry):
        rows = pl.ds(pl.multiple_of(index * STRIP, STRIP), STRIP)
        dx = px[rows, :] - across
        dy = py[rows, :] - along
        distance = jnp.sqrt(dx * dx + dy * dy + pz[rows, :])
        gain = area / distance
        opposite = -gain
        for line in range(lines):
            turn = distance * turns[line]
            turn = turn - jnp.round(turn)
            b = 0.25 - jnp.abs(turn)
            u = b * b
            cosine = polynomial(SINE, u) * b
            sine = polynomial(COSINE, u)
            signed = jnp.where(turn < 0.0, opposite, gain)
            out[0, line, rows, 0:LANES] = (signed * sine).astype(BF16)
            out[0, line, rows, LANES : 2 * LANES] = (gain * cosine).astype(BF16)
        return carry

    lax.fori_loop(0, out.shape[2] // STRIP, strip, 0)


def make_tiles(place, wave, blocks, mine, other, interpret=False):
    lines = wave.shape[0]
    sources = 4
    points = 4 * LANES
    last = mine.shape[1] // THIRDS - 1
    whole = pl.BlockSpec((3, LANES), lambda h, i, place, wave: (0, 0))
    panel = pl.BlockSpec(
        (1, THIRDS, LANES), lambda h, i, place, wave: (i * sources + place[2], last, 0)
    )
    return pl.pallas_call(
        tile_kernel,
        out_shape=jax.ShapeDtypeStruct((2 * sources, lines, points, 2 * LANES), BF16),
        grid_spec=pltpu.PrefetchScalarGridSpec(
            num_scalar_prefetch=2,
            grid=(2, sources),
            in_specs=[whole] * 4 + [panel] * 2,
            out_specs=pl.BlockSpec(
                (1, lines, points, 2 * LANES),
                lambda h, i, place, wave: (h * sources + i, 0, 0, 0),
            ),
            scratch_shapes=[pltpu.VMEM((points, LANES), F32)] * 3,
        ),
        cost_estimate=pl.CostEstimate(
            flops=8_000_000_000, bytes_accessed=8 << 20, transcendentals=0
        ),
        interpret=interpret,
        name="tiles",
    )(place, wave, *blocks, mine, other)


def velocity_kernel(place, mine, other, response, out, energy):
    a = mine[...].reshape(-1, LANES)
    b = other[...].reshape(-1, LANES)
    first = place[1] == 0
    real = jnp.where(first, a, b)
    imag = jnp.where(first, b, a)
    upper = jnp.concatenate([real, imag], axis=1)
    lower = jnp.concatenate([-imag, real], axis=1)
    total = jnp.dot(response[0, 0], upper, preferred_element_type=F32)
    total = total + jnp.dot(response[0, 1], lower, preferred_element_type=F32)
    rounded = total.astype(BF16)
    for copy in range(out.shape[0]):
        out[copy, 0] = rounded
    wide = rounded.astype(F32)
    squares = jnp.sum(wide * wide, axis=0, keepdims=True)
    energy[0] = squares[:, :LANES] + squares[:, LANES:]


def make_velocity(place, mine, other, response, copies, interpret=False):
    groups, _, cases = mine.shape
    lines, _, own, channels = response.shape
    force_spec = pl.BlockSpec((groups, channels // groups, cases), lambda l, place: (0, l, 0))
    return pl.pallas_call(
        velocity_kernel,
        out_shape=(
            jax.ShapeDtypeStruct((copies, lines, own, 2 * cases), BF16),
            jax.ShapeDtypeStruct((lines, 1, cases), F32),
        ),
        grid_spec=pltpu.PrefetchScalarGridSpec(
            num_scalar_prefetch=1,
            grid=(lines,),
            in_specs=[
                force_spec,
                force_spec,
                pl.BlockSpec((1, 2, own, channels), lambda l, place: (l, 0, 0, 0)),
            ],
            out_specs=(
                pl.BlockSpec((copies, 1, own, 2 * cases), lambda l, place: (0, l, 0, 0)),
                pl.BlockSpec((1, 1, cases), lambda l, place: (l, 0, 0)),
            ),
        ),
        cost_estimate=pl.CostEstimate(
            flops=2 * lines * own * 4 * channels * cases, bytes_accessed=3 << 20, transcendentals=0
        ),
        interpret=interpret,
        name="velocity",
    )(place, mine, other, response)


def pressure_kernel(tiles, near, far, out):
    sources = near.shape[0]
    total = None
    for half, block in enumerate((near, far)):
        for source in range(sources):
            upper = block[source, 0]
            lower = jnp.concatenate([-upper[:, LANES:], upper[:, :LANES]], axis=1)
            stacked = jnp.concatenate([upper, lower], axis=0)
            term = jnp.dot(tiles[half * sources + source, 0], stacked, preferred_element_type=F32)
            total = term if total is None else total + term
    out[:, 0] = total.astype(BF16).reshape(out.shape[0], out.shape[2], out.shape[3])


def make_partial(tiles, near, far, parts, interpret=False):
    chunks, lines, points, depth = tiles.shape
    sources, _, own, columns = near.shape
    spec = pl.BlockSpec((sources, 1, own, columns), lambda l: (0, l, 0, 0))
    return pl.pallas_call(
        pressure_kernel,
        out_shape=jax.ShapeDtypeStruct((parts, lines, points // parts, columns), BF16),
        grid=(lines,),
        in_specs=[pl.BlockSpec((chunks, 1, points, depth), lambda l: (0, l, 0, 0)), spec, spec],
        out_specs=pl.BlockSpec((parts, 1, points // parts, columns), lambda l: (0, l, 0, 0)),
        cost_estimate=pl.CostEstimate(
            flops=2 * lines * chunks * points * depth * columns,
            bytes_accessed=11 << 20,
            transcendentals=0,
        ),
        interpret=interpret,
        name="partial",
    )(tiles, near, far)


def level_kernel(rows, beside, out):
    lines = beside.shape[1]
    levels = []
    for line in range(lines):
        total = beside[0, line].astype(F32)
        for source in range(1, beside.shape[0]):
            total = total + beside[source, line].astype(F32)
        levels.append(total.reshape(-1, rows, total.shape[1]))
    out[...] = jnp.concatenate(levels, axis=1).astype(BF16)


def make_level(beside, rows, interpret=False):
    _, lines, share, columns = beside.shape
    return pl.pallas_call(
        functools.partial(level_kernel, rows),
        out_shape=jax.ShapeDtypeStruct((share // rows, lines * rows, columns), BF16),
        interpret=interpret,
        name="level",
    )(beside)


def finish_kernel(wave, column, energy, pressure, sums):
    lines = energy.shape[0]
    total = column[0].astype(F32)
    for source in range(1, column.shape[0]):
        total = total + column[source].astype(F32)
    rows = total.shape[0] // lines
    parts = [
        total[line * rows : (line + 1) * rows] * (wave[line] * (0.5 / math.pi))
        for line in range(lines)
    ]
    rounded = jnp.concatenate(parts, axis=0).astype(BF16)
    pressure[...] = rounded
    wide = rounded.astype(F32)
    wide = wide * wide
    both = wide[:, :LANES] + wide[:, LANES:]
    power = [
        jnp.sum(both[line * rows : (line + 1) * rows], axis=0, keepdims=True)
        for line in range(lines)
    ]
    table = jnp.concatenate([energy[line] for line in range(lines)] + power, axis=0)
    for copy in range(sums.shape[0]):
        sums[copy] = table


def make_finish(wave, column, energy, copies, interpret=False):
    lines, _, cases = energy.shape
    _, rows, columns = column.shape
    return pl.pallas_call(
        finish_kernel,
        out_shape=(
            jax.ShapeDtypeStruct((rows, columns), BF16),
            jax.ShapeDtypeStruct((copies, 2 * lines, cases), F32),
        ),
        in_specs=[
            pl.BlockSpec(memory_space=pltpu.SMEM),
            pl.BlockSpec(memory_space=pltpu.VMEM),
            pl.BlockSpec(memory_space=pltpu.VMEM),
        ],
        interpret=interpret,
        name="finish",
    )(wave, column, energy)


def fold_kernel(table, out):
    total = table[0]
    for source in range(1, table.shape[0]):
        total = total + table[source]
    for copy in range(out.shape[0]):
        out[copy] = total


def make_fold(table, copies, interpret=False):
    return pl.pallas_call(
        fold_kernel,
        out_shape=jax.ShapeDtypeStruct((copies,) + table.shape[1:], F32),
        interpret=interpret,
        name="fold",
    )(table)


def ratio_kernel(point_total, panel_total, table, out):
    lines = out.shape[0]
    total = table[0]
    for source in range(1, table.shape[0]):
        total = total + table[source]
    out[...] = total[lines:] / point_total / (total[:lines] / panel_total + 1e-06)


def make_ratio(table, point_total, panel_total, interpret=False):
    _, double, cases = table.shape
    return pl.pallas_call(
        functools.partial(ratio_kernel, point_total, panel_total),
        out_shape=jax.ShapeDtypeStruct((double // 2, cases), F32),
        interpret=interpret,
        name="ratio",
    )(table)


def exchange(array, axes):
    return lax.all_to_all(array, axes, 0, 0, tiled=True)


def gather(array, axes):
    size = lax.axis_size(axes)
    return exchange(jnp.broadcast_to(array[None], (size,) + array.shape), axes)


def shards(forces, response, panel_plane, panel_area, field_points, wavenumber):
    lines, _, channels, cases = forces.shape
    own = response.shape[2]
    rows = field_points.shape[1] // lax.axis_size(SURF)
    share = rows * lax.axis_size("y") * lax.axis_size("zl")
    place = jnp.stack([lax.axis_index(axis) for axis in ("zh", "c", "y")]).astype(jnp.int32)
    turn = lax.axis_size("zh")

    first = (lax.axis_index("zh") * 2 + lax.axis_index("c")) * own
    panels = lax.dynamic_slice_in_dim(panel_plane, first, own, 1)
    area = lax.dynamic_slice_in_dim(panel_area, first, own, 0)
    panels = jnp.concatenate([panels, area[None]], axis=0)
    high = lax.reduce_precision(panels, 8, 7)
    middle = lax.reduce_precision(panels - high, 8, 7)
    low = panels - high - middle
    thirds = jnp.stack([high, middle, low], axis=1).reshape(-1, own)
    thirds = jnp.pad(thirds, ((0, THIRDS - thirds.shape[0]), (0, 0))).astype(BF16)
    block = lax.dynamic_slice_in_dim(field_points, lax.axis_index("x") * share, share, 1)

    part = jnp.where(lax.axis_index("c") == 0, forces[:, 0], forces[:, 1])
    part = gather(part, "zl")
    part, block = lax.optimization_barrier((part, block))
    part = jnp.concatenate([part.transpose(1, 0, 2, 3).reshape(-1, cases), thirds], axis=0)
    mine = gather(part, ("x", "y"))
    blocks = [block] + [
        lax.ppermute(block, "zh", [(i, (i + step) % turn) for i in range(turn)])
        for step in range(1, turn)
    ]
    mine, blocks = lax.optimization_barrier((mine, blocks))
    other = lax.ppermute(mine, "c", SWAP)
    velocity, energy = make_velocity(place, mine, other, response, lax.axis_size("x"))
    velocity, tile_mine, tile_other = lax.optimization_barrier((velocity, mine, other))
    near = exchange(velocity, "x")
    tiles = make_tiles(place, wavenumber, blocks, tile_mine, tile_other)
    near, tiles = lax.optimization_barrier((near, tiles))
    far = lax.ppermute(near, "c", SWAP)
    partial = make_partial(tiles, near, far, lax.axis_size("y"))
    level = make_level(exchange(partial, "y"), rows)
    column = exchange(level, DEPTH)
    pressure, sums = make_finish(wavenumber, column, energy, lax.axis_size(LEVEL))
    sums = make_fold(exchange(sums, LEVEL), lax.axis_size(DEPTH))
    sums = exchange(sums, DEPTH)
    point_total = field_points.shape[1] * lax.axis_size(FIELD)
    panel_total = own * lax.axis_size(SURF + FIELD)
    efficiency = make_ratio(sums, point_total, panel_total)
    pressure = pressure.reshape(lines, rows, 2, cases).transpose(1, 0, 2, 3)
    return (pressure, efficiency)


def solution(mesh):
    grid = Mesh(np.asarray(mesh.devices).reshape(4, 4, 4, 4, 2), SURF + FIELD)
    return jax.shard_map(
        shards,
        mesh=grid,
        in_specs=(
            P(None, None, SURF, None),
            P(None, None, SURF + FIELD, None),
            P(None, SURF),
            P(SURF),
            P(None, FIELD),
            P(),
        ),
        out_specs=(P(FIELD + SURF, None, None, None), P()),
        check_vma=False,
    )
```

```python
import functools
import math

import jax
import jax.numpy as jnp
import numpy as np
from jax import lax
from jax.experimental import pallas as pl
from jax.experimental.pallas import tpu as pltpu
from jax.sharding import Mesh, PartitionSpec as P

SURF = ("x", "y", "zl")
FIELD = ("zh", "c")
DEPTH = ("zh", "zl")
LEVEL = ("x", "y", "c")
SWAP = [(0, 1), (1, 0)]
LANES = 128
STRIP = 32
GROUP = 16
BF16 = jnp.bfloat16
F32 = jnp.float32
INTERPRET = False


def fitted(function, count):
    top = 0.0625
    nodes = 0.5 * top * (1.0 - np.cos(np.pi * (np.arange(count) + 0.5) / count))
    powers = np.vander(nodes, count, increasing=True)
    return [float(value) for value in np.linalg.solve(powers, function(np.sqrt(nodes)))]


SINE = fitted(lambda b: np.sin(2.0 * np.pi * b) / b, 5)
COSINE = fitted(lambda b: np.cos(2.0 * np.pi * b), 5)


def polynomial(coefficients, u):
    total = u * coefficients[-1] + coefficients[-2]
    for value in coefficients[-3::-1]:
        total = total * u + value
    return total


def call(kernel, out, scalars, arrays, name, scratch=(), cost=None, pinned=9):
    single = not isinstance(out, (list, tuple))
    shapes = (out,) if single else tuple(out)
    if INTERPRET:
        results = tuple(jax.ShapeDtypeStruct(s.shape, s.dtype) for s in shapes)
    else:
        results = tuple(pltpu.VMEM(s.shape, s.dtype) for s in shapes)
        arrays = [
            pltpu.with_memory_space_constraint(array, pltpu.VMEM) if index < pinned else array
            for index, array in enumerate(arrays)
        ]
    outs = pl.pallas_call(
        kernel,
        out_shape=results,
        in_specs=[pl.BlockSpec(memory_space=pltpu.SMEM)] * len(scalars)
        + [
            pl.BlockSpec(memory_space=pltpu.VMEM) if index < pinned else pl.BlockSpec()
            for index in range(len(arrays))
        ],
        out_specs=tuple(pl.BlockSpec(memory_space=pltpu.VMEM) for _ in shapes),
        scratch_shapes=list(scratch),
        cost_estimate=cost,
        interpret=INTERPRET,
        name=name,
    )(*scalars, *arrays)
    return outs[0] if single else outs


def cost(flops, moved):
    return pl.CostEstimate(flops=flops, bytes_accessed=moved, transcendentals=0)


def thirds_of(row):
    high = row.astype(BF16).astype(F32)
    middle = (row - high).astype(BF16).astype(F32)
    return [high, middle, row - high - middle]


def start_kernel(place, forces, panel_plane, panel_area, field_points, out, panel_rows):
    zh, core, x, zl = (place(axis) for axis in ("zh", "c", "x", "zl"))
    lane = pl.multiple_of(x * LANES, LANES)
    row = field_points[2:3, pl.ds(lane, LANES)]
    for coordinate in (0, 1):
        other = field_points[coordinate : coordinate + 1, pl.ds(lane, LANES)]
        row = jnp.where(zl == coordinate, other, row)
    point = jnp.concatenate(thirds_of(row) + [jnp.zeros((5, LANES), F32)], axis=0)
    force = forces[zh, core].astype(F32)
    chunk = jnp.concatenate([force, point], axis=0).astype(BF16)
    for copy in range(out.shape[0]):
        out[copy] = chunk
    field = zh * 2 + core
    lane = pl.multiple_of(field * LANES, LANES)
    rows = thirds_of(panel_plane[0:1, pl.ds(lane, LANES)])
    rows += thirds_of(panel_plane[1:2, pl.ds(lane, LANES)])
    rows += thirds_of(panel_area[pl.ds(field, 1), :])
    rows = jnp.concatenate(rows + [jnp.zeros((GROUP - 9, LANES), F32)], axis=0)
    panel_rows[...] = rows.astype(BF16)


def make_start(place, forces, panel_plane, panel_area, field_points, copies):
    out = (
        jax.ShapeDtypeStruct((copies, GROUP, LANES), BF16),
        jax.ShapeDtypeStruct((GROUP, LANES), BF16),
    )
    arrays = [forces, panel_plane, panel_area, field_points]
    return call(functools.partial(start_kernel, place), out, [], arrays, "start", pinned=0)


def spread_kernel(column, panel_rows, out):
    rows = column[:, 0:8, :].astype(F32).reshape(-1, LANES).astype(BF16)
    rows = jnp.concatenate([rows, panel_rows[...]], axis=0)
    for copy in range(out.shape[0]):
        out[copy] = rows


def make_spread(column, panel_rows, copies):
    rows = column.shape[0] * 8 + GROUP
    out = jax.ShapeDtypeStruct((copies, rows, LANES), BF16)
    return call(spread_kernel, out, [], [column, panel_rows], "spread")


def velocity_kernel(place, mine, other, response, out, energy):
    first = place("c") == 0
    lines = response.shape[0]
    depth = response.shape[3] // mine.shape[0]
    for line in range(lines):
        rows = slice(line * depth, (line + 1) * depth)
        a = mine[:, rows, :].reshape(-1, LANES)
        b = other[:, rows, :].reshape(-1, LANES)
        real = jnp.where(first, a, b)
        imag = jnp.where(first, b, a)
        upper = jnp.concatenate([real, imag], axis=1)
        lower = jnp.concatenate([-imag, real], axis=1)
        total = jnp.dot(response[line, 0], upper, preferred_element_type=F32)
        total = total + jnp.dot(response[line, 1], lower, preferred_element_type=F32)
        rounded = total.astype(BF16)
        for copy in range(out.shape[0]):
            out[copy, line] = rounded
        wide = rounded.astype(F32)
        squares = jnp.sum(wide * wide, axis=0, keepdims=True)
        energy[line : line + 1, :] = squares[:, :LANES] + squares[:, LANES:]


def make_velocity(place, mine, other, response, copies):
    lines, _, own, channels = response.shape
    out = (
        jax.ShapeDtypeStruct((copies, lines, own, 2 * LANES), BF16),
        jax.ShapeDtypeStruct((lines, LANES), F32),
    )
    work = cost(8 * lines * own * channels * LANES, 3 << 20)
    return call(
        functools.partial(velocity_kernel, place),
        out,
        [],
        [mine, other, response],
        "velocity",
        cost=work,
        pinned=2,
    )


def tile_kernel(place, wave, column, mine, other, out, token, px, py, pz):
    lines = out.shape[1]
    sources = 4
    last = mine.shape[1] - GROUP
    half, source = pl.program_id(0), pl.program_id(1)

    @pl.when((half == 0) & (source == 0))
    def _():
        for slot in range(4):
            for coordinate, target in enumerate((px, py, pz)):
                part = column[slot * 4 + coordinate].astype(F32)
                row = part[8:9] + part[9:10] + part[10:11]
                if coordinate == 2:
                    row = row * row
                block = jnp.broadcast_to(row, (LANES, LANES)).T
                for piece in range(4):
                    start = piece * LANES + slot * STRIP
                    target[start : start + STRIP, :] = block[piece * STRIP : (piece + 1) * STRIP, :]
        token[...] = px[0:8, :]

    at = source * sources + place("y")
    thirds = jnp.where(
        half == 0,
        mine[at, last : last + GROUP, :].astype(F32),
        other[at, last : last + GROUP, :].astype(F32),
    )
    across = thirds[0:1] + thirds[1:2] + thirds[2:3]
    along = thirds[3:4] + thirds[4:5] + thirds[5:6]
    area = thirds[6:7] + thirds[7:8] + thirds[8:9]
    turns = [wave[line] * (0.5 / math.pi) for line in range(lines)]

    def strip(index, carry):
        rows = pl.ds(pl.multiple_of(index * STRIP, STRIP), STRIP)
        dx = px[rows, :] - across
        dy = py[rows, :] - along
        distance = jnp.sqrt(dx * dx + dy * dy + pz[rows, :])
        gain = area / distance
        opposite = -gain
        for line in range(lines):
            turn = distance * turns[line]
            turn = turn - jnp.round(turn)
            b = 0.25 - jnp.abs(turn)
            u = b * b
            cosine = polynomial(SINE, u) * b
            sine = polynomial(COSINE, u)
            signed = jnp.where(turn < 0.0, opposite, gain)
            out[0, line, rows, 0:LANES] = (signed * sine).astype(BF16)
            out[0, line, rows, LANES : 2 * LANES] = (gain * cosine).astype(BF16)
        return carry

    lax.fori_loop(0, out.shape[2] // STRIP, strip, 0)


def pinned_to_vmem(array):
    return array if INTERPRET else pltpu.with_memory_space_constraint(array, pltpu.VMEM)


def make_tiles(place, wave, column, mine, other):
    points = 4 * LANES
    lines = wave.shape[0]
    vmem = pl.BlockSpec(memory_space=pltpu.VMEM)
    return pl.pallas_call(
        functools.partial(tile_kernel, place),
        out_shape=(
            jax.ShapeDtypeStruct((8, lines, points, 2 * LANES), BF16),
            jax.ShapeDtypeStruct((8, LANES), F32),
        ),
        grid=(2, 4),
        in_specs=[pl.BlockSpec(memory_space=pltpu.SMEM), vmem, vmem, vmem],
        out_specs=(
            pl.BlockSpec((1, lines, points, 2 * LANES), lambda h, i: (h * 4 + i, 0, 0, 0)),
            pl.BlockSpec((8, LANES), lambda h, i: (0, 0)),
        ),
        scratch_shapes=[pltpu.VMEM((points, LANES), F32)] * 3,
        cost_estimate=cost(8_000_000_000, 8 << 20),
        interpret=INTERPRET,
        name="tiles",
    )(wave, *[pinned_to_vmem(array) for array in (column, mine, other)])


def terms(tiles, block, line):
    total = None
    for source in range(block.shape[0]):
        upper = block[source, line]
        lower = jnp.concatenate([-upper[:, LANES:], upper[:, :LANES]], axis=1)
        stacked = jnp.concatenate([upper, lower], axis=0)
        term = jnp.dot(tiles[source, 0], stacked, preferred_element_type=F32)
        total = term if total is None else total + term
    return total


def near_kernel(tiles, near, token, out):
    out[0] = terms(tiles, near, pl.program_id(0))


def far_kernel(tiles, far, held, out):
    parts, _, share, columns = out.shape
    total = held[0] + terms(tiles, far, pl.program_id(0))
    out[:, 0] = total.astype(BF16).reshape(parts, share, columns)


def make_near(tiles, near, token):
    chunks, lines, points, depth = tiles.shape
    columns = near.shape[3]
    vmem = pl.BlockSpec(memory_space=pltpu.VMEM)
    return pl.pallas_call(
        near_kernel,
        out_shape=jax.ShapeDtypeStruct((lines, points, columns), F32),
        grid=(lines,),
        in_specs=[
            pl.BlockSpec((chunks // 2, 1, points, depth), lambda l: (0, l, 0, 0)),
            vmem,
            vmem,
        ],
        out_specs=pl.BlockSpec((1, points, columns), lambda l: (l, 0, 0)),
        cost_estimate=cost(lines * chunks * points * depth * columns, 7 << 20),
        interpret=INTERPRET,
        name="near",
    )(tiles, pinned_to_vmem(near), pinned_to_vmem(token))


def make_far(tiles, far, held, parts):
    chunks, lines, points, depth = tiles.shape
    columns = far.shape[3]
    return pl.pallas_call(
        far_kernel,
        out_shape=jax.ShapeDtypeStruct((parts, lines, points // parts, columns), BF16),
        grid=(lines,),
        in_specs=[
            pl.BlockSpec((chunks // 2, 1, points, depth), lambda l: (1, l, 0, 0)),
            pl.BlockSpec(memory_space=pltpu.VMEM),
            pl.BlockSpec((1, points, columns), lambda l: (l, 0, 0)),
        ],
        out_specs=pl.BlockSpec((parts, 1, points // parts, columns), lambda l: (0, l, 0, 0)),
        cost_estimate=cost(lines * chunks * points * depth * columns, 8 << 20),
        interpret=INTERPRET,
        name="far",
    )(tiles, pinned_to_vmem(far), held)


def level_kernel(rows, beside, out):
    levels = []
    for line in range(beside.shape[1]):
        total = beside[0, line].astype(F32)
        for source in range(1, beside.shape[0]):
            total = total + beside[source, line].astype(F32)
        levels.append(total.reshape(-1, rows, total.shape[1]))
    out[...] = jnp.concatenate(levels, axis=1).astype(BF16)


def make_level(beside, rows):
    _, lines, share, columns = beside.shape
    out = jax.ShapeDtypeStruct((share // rows, lines * rows, columns), BF16)
    return call(functools.partial(level_kernel, rows), out, [], [beside], "level")


def finish_kernel(wave, column, energy, pressure, sums):
    lines = energy.shape[0]
    total = column[0].astype(F32)
    for source in range(1, column.shape[0]):
        total = total + column[source].astype(F32)
    rows = total.shape[0] // lines
    parts = [
        total[line * rows : (line + 1) * rows] * (wave[line] * (0.5 / math.pi))
        for line in range(lines)
    ]
    rounded = jnp.concatenate(parts, axis=0).astype(BF16)
    pressure[...] = rounded
    wide = rounded.astype(F32)
    wide = wide * wide
    both = wide[:, :LANES] + wide[:, LANES:]
    power = [
        jnp.sum(both[line * rows : (line + 1) * rows], axis=0, keepdims=True)
        for line in range(lines)
    ]
    table = jnp.concatenate([energy[...]] + power, axis=0)
    for copy in range(sums.shape[0]):
        sums[copy] = table


def make_finish(wave, column, energy, copies):
    lines, cases = energy.shape
    _, rows, columns = column.shape
    out = (
        jax.ShapeDtypeStruct((rows, columns), BF16),
        jax.ShapeDtypeStruct((copies, 2 * lines, cases), F32),
    )
    return call(finish_kernel, out, [wave], [column, energy], "finish")


def fold_kernel(table, out):
    total = table[0]
    for source in range(1, table.shape[0]):
        total = total + table[source]
    for copy in range(out.shape[0]):
        out[copy] = total


def make_fold(table, copies):
    out = jax.ShapeDtypeStruct((copies,) + table.shape[1:], F32)
    return call(fold_kernel, out, [], [table], "fold")


def exchange(array, axes):
    return lax.all_to_all(array, axes, 0, 0, tiled=True)


def shards(forces, response, panel_plane, panel_area, field_points, wavenumber):
    lines, _, channels, cases = forces.shape
    own = response.shape[2]
    rows = field_points.shape[1] // lax.axis_size(SURF)
    place = lax.axis_index

    area = panel_area.reshape(-1, own)
    column, panel_rows = make_start(
        place, forces, panel_plane, area, field_points, lax.axis_size(DEPTH)
    )
    column = exchange(column, DEPTH)
    mine = exchange(make_spread(column, panel_rows, lax.axis_size(("x", "y"))), ("x", "y"))
    other = lax.ppermute(mine, "c", SWAP)
    velocity, energy = make_velocity(place, mine, other, response, lax.axis_size("x"))
    energy, column, tile_mine, tile_other = lax.optimization_barrier(
        (energy, column, mine, other)
    )
    near = exchange(velocity, "x")
    tiles, token = make_tiles(place, wavenumber, column, tile_mine, tile_other)
    near, token = lax.optimization_barrier((near, token))
    far = lax.ppermute(near, "c", SWAP)
    partial = make_far(tiles, far, make_near(tiles, near, token), lax.axis_size("y"))
    level = make_level(exchange(partial, "y"), rows)
    column = exchange(level, DEPTH)
    pressure, sums = make_finish(wavenumber, column, energy, lax.axis_size(LEVEL))
    sums = make_fold(exchange(sums, LEVEL), lax.axis_size(DEPTH))
    sums = jnp.sum(exchange(sums, DEPTH), axis=0)
    point_total = field_points.shape[1] * lax.axis_size(FIELD)
    panel_total = own * lax.axis_size(SURF + FIELD)
    efficiency = sums[lines:] / point_total / (sums[:lines] / panel_total + 1e-06)
    pressure = pressure.reshape(lines, rows, 2, cases).transpose(1, 0, 2, 3)
    return (pressure, efficiency)


def solution(mesh):
    grid = Mesh(np.asarray(mesh.devices).reshape(4, 4, 4, 4, 2), SURF + FIELD)
    return jax.shard_map(
        shards,
        mesh=grid,
        in_specs=(
            P(None, None, SURF, None),
            P(None, None, SURF + FIELD, None),
            P(None, SURF),
            P(SURF),
            P(None, FIELD),
            P(),
        ),
        out_specs=(P(FIELD + SURF, None, None, None), P()),
        check_vma=False,
    )
```

```python
import functools
import math

import jax
import jax.numpy as jnp
import numpy as np
from jax import lax
from jax.experimental import pallas as pl
from jax.experimental.pallas import tpu as pltpu
from jax.sharding import Mesh, PartitionSpec as P

SURF = ("s", "zl")
FIELD = ("zh", "c")
DEPTH = ("zh", "zl")
LEVEL = ("s", "c")
SWAP = [(0, 1), (1, 0)]
LANES = 128
STRIP = 32
SIDE = 4
PAIRS = [(a, b) for a in range(2) for b in range(2)]
SQUARES = [[(2 * i + a) * SIDE + 2 * j + b for a, b in PAIRS] for i, j in PAIRS]
SHIFTED = [
    [(2 * i + a + 3) % SIDE * SIDE + (2 * j + b + 3) % SIDE for a, b in PAIRS] for i, j in PAIRS
]
GROUP = 16
BF16 = jnp.bfloat16
F32 = jnp.float32
INTERPRET = False


def fitted(function, count):
    top = 0.0625
    nodes = 0.5 * top * (1.0 - np.cos(np.pi * (np.arange(count) + 0.5) / count))
    powers = np.vander(nodes, count, increasing=True)
    return [float(value) for value in np.linalg.solve(powers, function(np.sqrt(nodes)))]


SINE = fitted(lambda b: np.sin(2.0 * np.pi * b) / b, 5)
COSINE = fitted(lambda b: np.cos(2.0 * np.pi * b), 5)


def polynomial(coefficients, u):
    total = u * coefficients[-1] + coefficients[-2]
    for value in coefficients[-3::-1]:
        total = total * u + value
    return total


def call(kernel, out, scalars, arrays, name, scratch=(), cost=None, pinned=9):
    single = not isinstance(out, (list, tuple))
    shapes = (out,) if single else tuple(out)
    if INTERPRET:
        results = tuple(jax.ShapeDtypeStruct(s.shape, s.dtype) for s in shapes)
    else:
        results = tuple(pltpu.VMEM(s.shape, s.dtype) for s in shapes)
        arrays = [
            pltpu.with_memory_space_constraint(array, pltpu.VMEM) if index < pinned else array
            for index, array in enumerate(arrays)
        ]
    outs = pl.pallas_call(
        kernel,
        out_shape=results,
        in_specs=[pl.BlockSpec(memory_space=pltpu.SMEM)] * len(scalars)
        + [
            pl.BlockSpec(memory_space=pltpu.VMEM) if index < pinned else pl.BlockSpec()
            for index in range(len(arrays))
        ],
        out_specs=tuple(pl.BlockSpec(memory_space=pltpu.VMEM) for _ in shapes),
        scratch_shapes=list(scratch),
        cost_estimate=cost,
        interpret=INTERPRET,
        name=name,
    )(*scalars, *arrays)
    return outs[0] if single else outs


def cost(flops, moved):
    return pl.CostEstimate(flops=flops, bytes_accessed=moved, transcendentals=0)


def thirds_of(row):
    high = row.astype(BF16).astype(F32)
    middle = (row - high).astype(BF16).astype(F32)
    return [high, middle, row - high - middle]


def start_kernel(place, forces, panel_plane, panel_area, field_points, out, panel_rows):
    zh, core, zl = (place(axis) for axis in ("zh", "c", "zl"))
    x, y = lax.div(place("s"), SIDE), lax.rem(place("s"), SIDE)
    x_first = lax.rem(2 * lax.div(lax.rem(x + 1, SIDE), 2) + 3, SIDE)
    y_first = lax.rem(2 * lax.div(lax.rem(y + 1, SIDE), 2) + 3, SIDE)
    piece = lax.broadcasted_iota(jnp.int32, (3, LANES), 1) // STRIP
    block = jnp.zeros((3, LANES), F32)
    for index, (a, b) in enumerate(PAIRS):
        lane = pl.multiple_of(lax.rem(x_first + a, SIDE) * LANES, LANES)
        shift = lax.rem(index + SIDE - lax.rem(y_first + b, SIDE), SIDE) * STRIP
        moved = pltpu.roll(field_points[:, pl.ds(lane, LANES)], shift, 1)
        block = jnp.where(piece == index, moved, block)
    row = block[2:3]
    for coordinate in (0, 1):
        row = jnp.where(zl == coordinate, block[coordinate : coordinate + 1], row)
    point = jnp.concatenate(thirds_of(row) + [jnp.zeros((5, LANES), F32)], axis=0)
    force = forces[zh, core].astype(F32)
    chunk = jnp.concatenate([force, point], axis=0).astype(BF16)
    for copy in range(out.shape[0]):
        out[copy] = chunk
    for half in range(2):
        field = zh * 2 + lax.rem(core + half, 2)
        lane = pl.multiple_of(field * LANES, LANES)
        rows = thirds_of(panel_plane[0:1, pl.ds(lane, LANES)])
        rows += thirds_of(panel_plane[1:2, pl.ds(lane, LANES)])
        rows += thirds_of(panel_area[pl.ds(field, 1), :])
        rows = jnp.concatenate(rows + [jnp.zeros((GROUP - 9, LANES), F32)], axis=0)
        panel_rows[half] = rows.astype(BF16)


def make_start(place, forces, panel_plane, panel_area, field_points, copies):
    out = (
        jax.ShapeDtypeStruct((copies, GROUP, LANES), BF16),
        jax.ShapeDtypeStruct((2, GROUP, LANES), BF16),
    )
    arrays = [forces, panel_plane, panel_area, field_points]
    return call(functools.partial(start_kernel, place), out, [], arrays, "start", pinned=0)


def spread_kernel(column, panel_rows, out):
    rows = column[:, 0:8, :].astype(F32).reshape(-1, LANES).astype(BF16)
    rows = jnp.concatenate([rows, panel_rows[0]], axis=0)
    for copy in range(out.shape[0]):
        out[copy] = rows


def make_spread(column, panel_rows, copies):
    rows = column.shape[0] * 8 + GROUP
    out = jax.ShapeDtypeStruct((copies, rows, LANES), BF16)
    return call(spread_kernel, out, [], [column, panel_rows], "spread")


def velocity_kernel(place, mine, other, response, out, energy):
    first = place("c") == 0
    lines = response.shape[0]
    depth = response.shape[3] // mine.shape[0]
    for line in range(lines):
        rows = slice(line * depth, (line + 1) * depth)
        a = mine[:, rows, :].reshape(-1, LANES)
        b = other[:, rows, :].reshape(-1, LANES)
        real = jnp.where(first, a, b)
        imag = jnp.where(first, b, a)
        upper = jnp.concatenate([real, imag], axis=1)
        lower = jnp.concatenate([-imag, real], axis=1)
        total = jnp.dot(response[line, 0], upper, preferred_element_type=F32)
        total = total + jnp.dot(response[line, 1], lower, preferred_element_type=F32)
        rounded = total.astype(BF16)
        for copy in range(out.shape[0]):
            out[copy, line] = rounded
        wide = rounded.astype(F32)
        squares = jnp.sum(wide * wide, axis=0, keepdims=True)
        energy[line : line + 1, :] = squares[:, :LANES] + squares[:, LANES:]


def make_velocity(place, mine, other, response, copies):
    lines, _, own, channels = response.shape
    out = (
        jax.ShapeDtypeStruct((copies, lines, own, 2 * LANES), BF16),
        jax.ShapeDtypeStruct((lines, LANES), F32),
    )
    work = cost(8 * lines * own * channels * LANES, 3 << 20)
    return call(
        functools.partial(velocity_kernel, place),
        out,
        [],
        [mine, other, response],
        "velocity",
        cost=work,
        pinned=2,
    )


def square_place(place):
    x, y = lax.div(place("s"), SIDE), lax.rem(place("s"), SIDE)
    return 2 * lax.rem(x, 2) + lax.rem(y, 2), 2 * lax.div(x, 2) * SIDE + 2 * lax.div(y, 2)


def set_points(column, token, px, py, pz):
    for slot in range(4):
        for coordinate, target in enumerate((px, py, pz)):
            part = column[slot * 4 + coordinate].astype(F32)
            row = part[8:9] + part[9:10] + part[10:11]
            if coordinate == 2:
                row = row * row
            block = jnp.broadcast_to(row, (LANES, LANES)).T
            for piece in range(4):
                start = piece * LANES + slot * STRIP
                target[start : start + STRIP, :] = block[piece * STRIP : (piece + 1) * STRIP, :]
    token[...] = px[0:8, :]


def own_kernel(wave, column, panel_rows, out, token, px, py, pz):
    @pl.when(pl.program_id(0) == 0)
    def _():
        set_points(column, token, px, py, pz)

    fill_tiles(wave, panel_rows[pl.program_id(0)].astype(F32), out, px, py, pz)


def rest_kernel(place, wave, column, mine, other, before, out, token, px, py, pz):
    last = mine.shape[1] - GROUP
    half, step = pl.program_id(0), pl.program_id(1)

    @pl.when((half == 0) & (step == 0))
    def _():
        set_points(column, token, px, py, pz)

    own, corner = square_place(place)
    source = jnp.bitwise_xor(own, step + 1)
    at = corner + lax.div(source, 2) * SIDE + lax.rem(source, 2)
    thirds = jnp.where(
        half == 0,
        mine[at, last : last + GROUP, :].astype(F32),
        other[at, last : last + GROUP, :].astype(F32),
    )
    fill_tiles(wave, thirds, out, px, py, pz)


def fill_tiles(wave, thirds, out, px, py, pz):
    lines = out.shape[1]
    across = thirds[0:1] + thirds[1:2] + thirds[2:3]
    along = thirds[3:4] + thirds[4:5] + thirds[5:6]
    area = thirds[6:7] + thirds[7:8] + thirds[8:9]
    turns = [wave[line] * (0.5 / math.pi) for line in range(lines)]

    def strip(index, carry):
        rows = pl.ds(pl.multiple_of(index * STRIP, STRIP), STRIP)
        dx = px[rows, :] - across
        dy = py[rows, :] - along
        distance = jnp.sqrt(dx * dx + dy * dy + pz[rows, :])
        gain = area / distance
        opposite = -gain
        for line in range(lines):
            turn = distance * turns[line]
            turn = turn - jnp.round(turn)
            b = 0.25 - jnp.abs(turn)
            u = b * b
            cosine = polynomial(SINE, u) * b
            sine = polynomial(COSINE, u)
            signed = jnp.where(turn < 0.0, opposite, gain)
            out[0, line, rows, 0:LANES] = (signed * sine).astype(BF16)
            out[0, line, rows, LANES : 2 * LANES] = (gain * cosine).astype(BF16)
        return carry

    lax.fori_loop(0, out.shape[2] // STRIP, strip, 0)


def pinned_to_vmem(array):
    return array if INTERPRET else pltpu.with_memory_space_constraint(array, pltpu.VMEM)


def make_tiles(kernel, wave, arrays, grid, name, after=()):
    points = 4 * LANES
    lines = wave.shape[0]
    vmem = pl.BlockSpec(memory_space=pltpu.VMEM)
    steps = math.prod(grid)
    inner = grid[1] if len(grid) == 2 else 1
    return pl.pallas_call(
        kernel,
        out_shape=(
            jax.ShapeDtypeStruct((steps, lines, points, 2 * LANES), BF16),
            jax.ShapeDtypeStruct((8, LANES), F32),
        ),
        grid=grid,
        in_specs=[pl.BlockSpec(memory_space=pltpu.SMEM)]
        + [vmem] * len(arrays)
        + [pl.BlockSpec(memory_space=pl.ANY)] * len(after),
        out_specs=(
            pl.BlockSpec(
                (1, lines, points, 2 * LANES),
                lambda h, i=0: (h * inner + i, 0, 0, 0),
            ),
            pl.BlockSpec((8, LANES), lambda *_: (0, 0)),
        ),
        scratch_shapes=[pltpu.VMEM((points, LANES), F32)] * 3,
        cost_estimate=cost(steps * 1_000_000_000, steps << 20),
        interpret=INTERPRET,
        name=name,
    )(wave, *[pinned_to_vmem(array) for array in arrays], *after)


def make_own(wave, column, panel_rows):
    return make_tiles(own_kernel, wave, [column, panel_rows], (2,), "own")


def make_rest(place, wave, column, mine, other, before):
    kernel = functools.partial(rest_kernel, place)
    return make_tiles(kernel, wave, [column, mine, other], (2, 3), "rest", (before,))


def terms(place, tiles, block, line):
    own, _ = square_place(place)
    total = None
    for step in range(block.shape[0]):
        upper = block[jnp.bitwise_xor(own, step), line]
        lower = jnp.concatenate([-upper[:, LANES:], upper[:, :LANES]], axis=1)
        stacked = jnp.concatenate([upper, lower], axis=0)
        term = jnp.dot(tiles[step][0, 0], stacked, preferred_element_type=F32)
        total = term if total is None else total + term
    return total


def near_kernel(place, a, b, c, d, near, token, out):
    out[0] = terms(place, (a, b, c, d), near, pl.program_id(0))


def far_kernel(place, a, b, c, d, far, held, out):
    parts, _, share, columns = out.shape
    total = held[0] + terms(place, (a, b, c, d), far, pl.program_id(0))
    out[:, 0] = total.astype(BF16).reshape(parts, share, columns)


def tile_specs(half, points, depth):
    specs = [pl.BlockSpec((1, 1, points, depth), lambda l: (half, l, 0, 0))]
    for step in range(3):
        at = half * 3 + step
        specs.append(pl.BlockSpec((1, 1, points, depth), lambda l, at=at: (at, l, 0, 0)))
    return specs


def make_near(place, own, rest, near, token):
    _, lines, points, depth = own.shape
    columns = near.shape[3]
    return pl.pallas_call(
        functools.partial(near_kernel, place),
        out_shape=jax.ShapeDtypeStruct((lines, points, columns), F32),
        grid=(lines,),
        in_specs=tile_specs(0, points, depth)
        + [pl.BlockSpec(memory_space=pltpu.VMEM), pl.BlockSpec(memory_space=pl.ANY)],
        out_specs=pl.BlockSpec((1, points, columns), lambda l: (l, 0, 0)),
        cost_estimate=cost(8 * lines * points * depth * columns, 7 << 20),
        interpret=INTERPRET,
        name="near",
    )(own, rest, rest, rest, pinned_to_vmem(near), token)


def make_far(place, own, rest, far, held, parts):
    _, lines, points, depth = own.shape
    columns = far.shape[3]
    return pl.pallas_call(
        functools.partial(far_kernel, place),
        out_shape=jax.ShapeDtypeStruct((parts, lines, points // parts, columns), BF16),
        grid=(lines,),
        in_specs=tile_specs(1, points, depth)
        + [
            pl.BlockSpec(memory_space=pltpu.VMEM),
            pl.BlockSpec((1, points, columns), lambda l: (l, 0, 0)),
        ],
        out_specs=pl.BlockSpec((parts, 1, points // parts, columns), lambda l: (0, l, 0, 0)),
        cost_estimate=cost(8 * lines * points * depth * columns, 8 << 20),
        interpret=INTERPRET,
        name="far",
    )(own, rest, rest, rest, pinned_to_vmem(far), held)


def level_kernel(rows, beside, out):
    levels = []
    for line in range(beside.shape[1]):
        total = beside[0, line].astype(F32)
        for source in range(1, beside.shape[0]):
            total = total + beside[source, line].astype(F32)
        levels.append(total.reshape(-1, rows, total.shape[1]))
    out[...] = jnp.concatenate(levels, axis=1).astype(BF16)


def make_level(beside, rows):
    _, lines, share, columns = beside.shape
    out = jax.ShapeDtypeStruct((share // rows, lines * rows, columns), BF16)
    return call(functools.partial(level_kernel, rows), out, [], [beside], "level")


def finish_kernel(wave, column, energy, pressure, sums):
    lines = energy.shape[0]
    total = column[0].astype(F32)
    for source in range(1, column.shape[0]):
        total = total + column[source].astype(F32)
    rows = total.shape[0] // lines
    parts = [
        total[line * rows : (line + 1) * rows] * (wave[line] * (0.5 / math.pi))
        for line in range(lines)
    ]
    rounded = jnp.concatenate(parts, axis=0).astype(BF16)
    pressure[...] = rounded
    wide = rounded.astype(F32)
    wide = wide * wide
    both = wide[:, :LANES] + wide[:, LANES:]
    power = [
        jnp.sum(both[line * rows : (line + 1) * rows], axis=0, keepdims=True)
        for line in range(lines)
    ]
    table = jnp.concatenate([energy[...]] + power, axis=0)
    for copy in range(sums.shape[0]):
        sums[copy] = table


def make_finish(wave, column, energy, copies):
    lines, cases = energy.shape
    _, rows, columns = column.shape
    out = (
        jax.ShapeDtypeStruct((rows, columns), BF16),
        jax.ShapeDtypeStruct((copies, 2 * lines, cases), F32),
    )
    return call(finish_kernel, out, [wave], [column, energy], "finish")


def fold_kernel(table, out):
    total = table[0]
    for source in range(1, table.shape[0]):
        total = total + table[source]
    for copy in range(out.shape[0]):
        out[copy] = total


def make_fold(table, copies):
    out = jax.ShapeDtypeStruct((copies,) + table.shape[1:], F32)
    return call(fold_kernel, out, [], [table], "fold")


def exchange(array, axes, groups=None):
    return lax.all_to_all(array, axes, 0, 0, tiled=True, axis_index_groups=groups)


def shards(forces, response, panel_plane, panel_area, field_points, wavenumber):
    lines, _, channels, cases = forces.shape
    own = response.shape[2]
    rows = field_points.shape[1] // lax.axis_size(SURF)
    place = lax.axis_index

    area = panel_area.reshape(-1, own)
    column, panel_rows = make_start(
        place, forces, panel_plane, area, field_points, lax.axis_size(DEPTH)
    )
    column = exchange(column, DEPTH)
    mine = exchange(make_spread(column, panel_rows, lax.axis_size("s")), "s")
    own_tiles, token = make_own(wavenumber, column, panel_rows)
    mine, column, token = lax.optimization_barrier((mine, column, token))
    other = lax.ppermute(mine, "c", SWAP)
    velocity, energy = make_velocity(place, mine, other, response, len(PAIRS))
    energy, column, tile_mine, tile_other, token = lax.optimization_barrier(
        (energy, column, mine, other, token)
    )
    near = exchange(velocity, "s", SQUARES)
    rest_tiles, token = make_rest(place, wavenumber, column, tile_mine, tile_other, token)
    near, token = lax.optimization_barrier((near, token))
    far = lax.ppermute(near, "c", SWAP)
    held = make_near(place, own_tiles, rest_tiles, near, token)
    partial = make_far(place, own_tiles, rest_tiles, far, held, len(PAIRS))
    beside = exchange(partial, "s", SHIFTED)
    level = make_level(beside, rows)
    column = exchange(level, DEPTH)
    pressure, sums = make_finish(wavenumber, column, energy, lax.axis_size(LEVEL))
    sums = make_fold(exchange(sums, LEVEL), lax.axis_size(DEPTH))
    sums = jnp.sum(exchange(sums, DEPTH), axis=0)
    point_total = field_points.shape[1] * lax.axis_size(FIELD)
    panel_total = own * lax.axis_size(SURF + FIELD)
    efficiency = sums[lines:] / point_total / (sums[:lines] / panel_total + 1e-06)
    pressure = pressure.reshape(lines, rows, 2, cases).transpose(1, 0, 2, 3)
    return (pressure, efficiency)


def solution(mesh):
    grid = Mesh(np.asarray(mesh.devices).reshape(16, 4, 4, 2), SURF + FIELD)
    return jax.shard_map(
        shards,
        mesh=grid,
        in_specs=(
            P(None, None, SURF, None),
            P(None, None, SURF + FIELD, None),
            P(None, SURF),
            P(SURF),
            P(None, FIELD),
            P(),
        ),
        out_specs=(P(FIELD + SURF, None, None, None), P()),
        check_vma=False,
    )
```

```python
import functools
import math

import jax
import jax.numpy as jnp
import numpy as np
from jax import lax
from jax.experimental import pallas as pl
from jax.experimental.pallas import tpu as pltpu
from jax.sharding import Mesh, PartitionSpec as P

SURF = ("s", "zl")
FIELD = ("zh", "c")
DEPTH = ("zh", "zl")
LEVEL = ("s", "c")
SWAP = [(0, 1), (1, 0)]
LANES = 128
STRIP = 32
SIDE = 4
GRID = ("s", "zl", "zh", "c")


def rings(first):
    groups = []
    for zl in range(SIDE):
        for zh in range(SIDE):
            for core in range(2):
                for fixed in range(SIDE):
                    chips = [
                        moving * SIDE + fixed if core == first else fixed * SIDE + moving
                        for moving in range(SIDE)
                    ]
                    groups.append([((chip * SIDE + zl) * SIDE + zh) * 2 + core for chip in chips])
    return groups


GATHER = rings(0)
REDUCE = rings(1)
GROUP = 16
BF16 = jnp.bfloat16
F32 = jnp.float32
INTERPRET = False


def fitted(function, count):
    top = 0.0625
    nodes = 0.5 * top * (1.0 - np.cos(np.pi * (np.arange(count) + 0.5) / count))
    powers = np.vander(nodes, count, increasing=True)
    return [float(value) for value in np.linalg.solve(powers, function(np.sqrt(nodes)))]


SINE = fitted(lambda b: np.sin(2.0 * np.pi * b) / b, 5)
COSINE = fitted(lambda b: np.cos(2.0 * np.pi * b), 5)


def polynomial(coefficients, u):
    total = u * coefficients[-1] + coefficients[-2]
    for value in coefficients[-3::-1]:
        total = total * u + value
    return total


def call(kernel, out, scalars, arrays, name, scratch=(), cost=None, pinned=9):
    single = not isinstance(out, (list, tuple))
    shapes = (out,) if single else tuple(out)
    if INTERPRET:
        results = tuple(jax.ShapeDtypeStruct(s.shape, s.dtype) for s in shapes)
    else:
        results = tuple(pltpu.VMEM(s.shape, s.dtype) for s in shapes)
        arrays = [
            pltpu.with_memory_space_constraint(array, pltpu.VMEM) if index < pinned else array
            for index, array in enumerate(arrays)
        ]
    outs = pl.pallas_call(
        kernel,
        out_shape=results,
        in_specs=[pl.BlockSpec(memory_space=pltpu.SMEM)] * len(scalars)
        + [
            pl.BlockSpec(memory_space=pltpu.VMEM) if index < pinned else pl.BlockSpec()
            for index in range(len(arrays))
        ],
        out_specs=tuple(pl.BlockSpec(memory_space=pltpu.VMEM) for _ in shapes),
        scratch_shapes=list(scratch),
        cost_estimate=cost,
        interpret=INTERPRET,
        name=name,
    )(*scalars, *arrays)
    return outs[0] if single else outs


def cost(flops, moved):
    return pl.CostEstimate(flops=flops, bytes_accessed=moved, transcendentals=0)


def thirds_of(row):
    high = row.astype(BF16).astype(F32)
    middle = (row - high).astype(BF16).astype(F32)
    return [high, middle, row - high - middle]


def start_kernel(place, forces, panel_plane, panel_area, field_points, out, panel_rows):
    zh, core, zl = (place(axis) for axis in ("zh", "c", "zl"))
    x, y = lax.div(place("s"), SIDE), lax.rem(place("s"), SIDE)
    along_y = field_points[:, pl.ds(pl.multiple_of(x * LANES, LANES), LANES)]
    piece = lax.broadcasted_iota(jnp.int32, (3, LANES), 1) // STRIP
    along_x = jnp.zeros((3, LANES), F32)
    for index in range(SIDE):
        shift = lax.rem(index + SIDE - y, SIDE) * STRIP
        moved = pltpu.roll(field_points[:, index * LANES : (index + 1) * LANES], shift, 1)
        along_x = jnp.where(piece == index, moved, along_x)
    point = []
    for block in (
        jnp.where(core == 0, along_y, along_x),
        jnp.where(core == 0, along_x, along_y),
    ):
        row = block[2:3]
        for coordinate in (0, 1):
            row = jnp.where(zl == coordinate, block[coordinate : coordinate + 1], row)
        point += thirds_of(row)
    point = jnp.concatenate(point + [jnp.zeros((2, LANES), F32)], axis=0)
    force = forces[zh, core].astype(F32)
    chunk = jnp.concatenate([force, point], axis=0).astype(BF16)
    for copy in range(out.shape[0]):
        out[copy] = chunk
    for half in range(2):
        field = zh * 2 + lax.rem(core + half, 2)
        lane = pl.multiple_of(field * LANES, LANES)
        rows = thirds_of(panel_plane[0:1, pl.ds(lane, LANES)])
        rows += thirds_of(panel_plane[1:2, pl.ds(lane, LANES)])
        rows += thirds_of(panel_area[pl.ds(field, 1), :])
        rows = jnp.concatenate(rows + [jnp.zeros((GROUP - 9, LANES), F32)], axis=0)
        panel_rows[half] = rows.astype(BF16)


def make_start(place, forces, panel_plane, panel_area, field_points, copies):
    out = (
        jax.ShapeDtypeStruct((copies, GROUP, LANES), BF16),
        jax.ShapeDtypeStruct((2, GROUP, LANES), BF16),
    )
    arrays = [forces, panel_plane, panel_area, field_points]
    return call(functools.partial(start_kernel, place), out, [], arrays, "start", pinned=0)


def spread_kernel(column, panel_rows, out):
    rows = column[:, 0:8, :].astype(F32).reshape(-1, LANES).astype(BF16)
    rows = jnp.concatenate([rows, panel_rows[0]], axis=0)
    for copy in range(out.shape[0]):
        out[copy] = rows


def make_spread(column, panel_rows, copies):
    rows = column.shape[0] * 8 + GROUP
    out = jax.ShapeDtypeStruct((copies, rows, LANES), BF16)
    return call(spread_kernel, out, [], [column, panel_rows], "spread")


def velocity_kernel(place, mine, other, response, keep, give, energy):
    core = place("c")
    lines = response.shape[0]
    depth = response.shape[3] // mine.shape[0]
    for line in range(lines):
        rows = slice(line * depth, (line + 1) * depth)
        a = mine[:, rows, :].reshape(-1, LANES)
        b = other[:, rows, :].reshape(-1, LANES)
        real = jnp.where(core == 0, a, b)
        imag = jnp.where(core == 0, b, a)
        upper = jnp.concatenate([real, imag], axis=1)
        lower = jnp.concatenate([-imag, real], axis=1)
        total = jnp.dot(response[line, 0], upper, preferred_element_type=F32)
        total = total + jnp.dot(response[line, 1], lower, preferred_element_type=F32)
        rounded = total.astype(BF16)
        half, at = divmod(line, lines // 2)

        @pl.when(core == half)
        def _():
            keep[at] = rounded

        @pl.when(core != half)
        def _():
            give[at] = rounded

        wide = rounded.astype(F32)
        squares = jnp.sum(wide * wide, axis=0, keepdims=True)
        energy[line : line + 1, :] = squares[:, :LANES] + squares[:, LANES:]


def make_velocity(place, mine, other, response):
    lines, _, own, channels = response.shape
    half = jax.ShapeDtypeStruct((lines // 2, own, 2 * LANES), BF16)
    out = (half, half, jax.ShapeDtypeStruct((lines, LANES), F32))
    work = cost(8 * lines * own * channels * LANES, 3 << 20)
    kernel = functools.partial(velocity_kernel, place)
    arrays = [mine, other, response]
    return call(kernel, out, [], arrays, "velocity", cost=work, pinned=2)


def pack_kernel(keep, got, out):
    for copy in range(out.shape[0]):
        out[copy, 0] = keep[...]
        out[copy, 1] = got[...]


def make_pack(keep, got):
    out = jax.ShapeDtypeStruct((SIDE, 2) + keep.shape, BF16)
    return call(pack_kernel, out, [], [keep, got], "pack")


def ring_place(place):
    x, y = lax.div(place("s"), SIDE), lax.rem(place("s"), SIDE)
    first = place("c") == 0
    return jnp.where(first, x, y), jnp.where(first, y, x * SIDE), jnp.where(first, SIDE, 1)


def set_points(column, partner, token, px, py, pz):
    for half, (array, base) in enumerate(((column, 8), (partner, 11))):
        for slot in range(4):
            for coordinate, target in enumerate((px, py, pz)):
                part = array[slot * 4 + coordinate].astype(F32)
                row = part[base : base + 1] + part[base + 1 : base + 2] + part[base + 2 : base + 3]
                if coordinate == 2:
                    row = row * row
                block = jnp.broadcast_to(row, (LANES, LANES)).T
                for piece in range(SIDE):
                    start = (piece * 2 + half) * LANES + slot * STRIP
                    target[start : start + STRIP, :] = block[piece * STRIP : (piece + 1) * STRIP, :]
    token[...] = px[0:8, :]


def own_kernel(place, wave, column, partner, panel_rows, out, token, px, py, pz):
    @pl.when(pl.program_id(0) == 0)
    def _():
        set_points(column, partner, token, px, py, pz)

    fill_tiles(place, wave, panel_rows[pl.program_id(0)].astype(F32), out, px, py, pz)


def rest_kernel(place, wave, column, partner, mine, other, before, out, token, px, py, pz):
    last = mine.shape[1] - GROUP
    half, step = pl.program_id(0), pl.program_id(1)

    @pl.when((half == 0) & (step == 0))
    def _():
        set_points(column, partner, token, px, py, pz)

    own, origin, stride = ring_place(place)
    at = origin + stride * jnp.bitwise_xor(own, step + 1)
    thirds = jnp.where(
        half == 0,
        mine[at, last : last + GROUP, :].astype(F32),
        other[at, last : last + GROUP, :].astype(F32),
    )
    fill_tiles(place, wave, thirds, out, px, py, pz)


def fill_tiles(place, wave, thirds, out, px, py, pz):
    lines = out.shape[1]
    across = thirds[0:1] + thirds[1:2] + thirds[2:3]
    along = thirds[3:4] + thirds[4:5] + thirds[5:6]
    area = thirds[6:7] + thirds[7:8] + thirds[8:9]
    turns = [wave[place("c") * lines + line] * (0.5 / math.pi) for line in range(lines)]

    def strip(index, carry):
        rows = pl.ds(pl.multiple_of(index * STRIP, STRIP), STRIP)
        dx = px[rows, :] - across
        dy = py[rows, :] - along
        distance = jnp.sqrt(dx * dx + dy * dy + pz[rows, :])
        gain = area / distance
        opposite = -gain
        for line in range(lines):
            turn = distance * turns[line]
            turn = turn - jnp.round(turn)
            b = 0.25 - jnp.abs(turn)
            u = b * b
            cosine = polynomial(SINE, u) * b
            sine = polynomial(COSINE, u)
            signed = jnp.where(turn < 0.0, opposite, gain)
            out[0, line, rows, 0:LANES] = (signed * sine).astype(BF16)
            out[0, line, rows, LANES : 2 * LANES] = (gain * cosine).astype(BF16)
        return carry

    lax.fori_loop(0, out.shape[2] // STRIP, strip, 0)


def pinned_to_vmem(array):
    return array if INTERPRET else pltpu.with_memory_space_constraint(array, pltpu.VMEM)


def make_tiles(kernel, wave, arrays, grid, name, after=()):
    points = 8 * LANES
    lines = wave.shape[0] // 2
    vmem = pl.BlockSpec(memory_space=pltpu.VMEM)
    steps = math.prod(grid)
    inner = grid[1] if len(grid) == 2 else 1
    return pl.pallas_call(
        kernel,
        out_shape=(
            jax.ShapeDtypeStruct((steps, lines, points, 2 * LANES), BF16),
            jax.ShapeDtypeStruct((8, LANES), F32),
        ),
        grid=grid,
        in_specs=[pl.BlockSpec(memory_space=pltpu.SMEM)]
        + [vmem] * len(arrays)
        + [pl.BlockSpec(memory_space=pl.ANY)] * len(after),
        out_specs=(
            pl.BlockSpec(
                (1, lines, points, 2 * LANES),
                lambda h, i=0: (h * inner + i, 0, 0, 0),
            ),
            pl.BlockSpec((8, LANES), lambda *_: (0, 0)),
        ),
        scratch_shapes=[pltpu.VMEM((points, LANES), F32)] * 3,
        cost_estimate=cost(steps * 1_000_000_000, steps << 20),
        interpret=INTERPRET,
        name=name,
    )(wave, *[pinned_to_vmem(array) for array in arrays], *after)


def make_own(place, wave, column, partner, panel_rows):
    kernel = functools.partial(own_kernel, place)
    return make_tiles(kernel, wave, [column, partner, panel_rows], (2,), "own")


def make_rest(place, wave, column, partner, mine, other, before):
    kernel = functools.partial(rest_kernel, place)
    arrays = [column, partner, mine, other]
    return make_tiles(kernel, wave, arrays, (2, 3), "rest", (before,))


def partial_kernel(place, *refs):
    tiles, near, out = refs[:8], refs[8], refs[-1]
    line = pl.program_id(0)
    own, _, _ = ring_place(place)
    total = None
    for half in range(2):
        for step in range(SIDE):
            upper = near[jnp.bitwise_xor(own, step), half, line]
            lower = jnp.concatenate([-upper[:, LANES:], upper[:, :LANES]], axis=1)
            stacked = jnp.concatenate([upper, lower], axis=0)
            tile = tiles[half * SIDE + step][0, 0]
            term = jnp.dot(tile, stacked, preferred_element_type=F32)
            total = term if total is None else total + term
    parts, _, share, columns = out.shape
    out[:, 0] = total.astype(BF16).reshape(parts, share, columns)


def make_partial(place, own, rest, near):
    _, lines, points, depth = own.shape
    columns = near.shape[-1]
    step_rows = points // 2
    share = points // SIDE
    specs = []
    for half in range(2):
        for step in range(SIDE):
            at = half if step == 0 else half * 3 + step - 1
            specs.append(
                pl.BlockSpec((1, 1, step_rows, depth), lambda l, i, at=at: (at, l, i, 0))
            )
    return pl.pallas_call(
        functools.partial(partial_kernel, place),
        out_shape=jax.ShapeDtypeStruct((SIDE, lines, share, columns), BF16),
        grid=(lines, 2),
        in_specs=specs + [pl.BlockSpec(memory_space=pltpu.VMEM)],
        out_specs=pl.BlockSpec((2, 1, share, columns), lambda l, i: (i, l, 0, 0)),
        cost_estimate=cost(16 * lines * points * depth * columns, 10 << 20),
        interpret=INTERPRET,
        name="partial",
    )(*(([own] + [rest] * 3) * 2), pinned_to_vmem(near))


def level_kernel(rows, beside, out):
    levels = []
    for line in range(beside.shape[1]):
        total = beside[0, line].astype(F32)
        for source in range(1, beside.shape[0]):
            total = total + beside[source, line].astype(F32)
        share = total.shape[0] // 2
        for half in range(2):
            part = total[half * share : (half + 1) * share]
            levels.append(part.reshape(-1, rows, total.shape[1]))
    out[...] = jnp.concatenate(levels, axis=1).astype(BF16)


def make_level(beside, rows):
    _, lines, share, columns = beside.shape
    out = jax.ShapeDtypeStruct((share // (2 * rows), lines * 2 * rows, columns), BF16)
    return call(functools.partial(level_kernel, rows), out, [], [beside], "level")


def finish_kernel(place, wave, column, energy, keep, give, sums):
    lines = energy.shape[0]
    core = place("c")
    total = column[0].astype(F32)
    for source in range(1, column.shape[0]):
        total = total + column[source].astype(F32)
    half = lines // 2
    share = total.shape[0] // half
    rows = share // 2
    parts = [
        total[line * share : (line + 1) * share] * (wave[core * half + line] * (0.5 / math.pi))
        for line in range(half)
    ]
    rounded = jnp.concatenate(parts, axis=0).astype(BF16)
    wide = rounded.astype(F32)
    for line in range(half):
        start = line * share
        keep[line * rows : (line + 1) * rows, :] = wide[start : start + rows].astype(BF16)
        give[line * rows : (line + 1) * rows, :] = wide[start + rows : start + share].astype(BF16)
    wide = wide * wide
    both = wide[:, :LANES] + wide[:, LANES:]
    power = [
        jnp.sum(both[line * share : (line + 1) * share], axis=0, keepdims=True)
        for line in range(half)
    ]
    nothing = jnp.zeros_like(power[0])
    power = [jnp.where(core == line // half, power[line % half], nothing) for line in range(lines)]
    table = jnp.concatenate([energy[...]] + power, axis=0)
    for copy in range(sums.shape[0]):
        sums[copy] = table


def make_finish(place, wave, column, energy, copies):
    lines, cases = energy.shape
    _, rows, columns = column.shape
    half = jax.ShapeDtypeStruct((rows // 2, columns), BF16)
    out = (half, half, jax.ShapeDtypeStruct((copies, 2 * lines, cases), F32))
    kernel = functools.partial(finish_kernel, place)
    return call(kernel, out, [wave], [column, energy], "finish")


def fold_kernel(table, out):
    total = table[0]
    for source in range(1, table.shape[0]):
        total = total + table[source]
    for copy in range(out.shape[0]):
        out[copy] = total


def make_fold(table, copies):
    out = jax.ShapeDtypeStruct((copies,) + table.shape[1:], F32)
    return call(fold_kernel, out, [], [table], "fold")


def exchange(array, axes, groups=None):
    return lax.all_to_all(array, axes, 0, 0, tiled=True, axis_index_groups=groups)


def shards(forces, response, panel_plane, panel_area, field_points, wavenumber):
    lines, _, channels, cases = forces.shape
    own = response.shape[2]
    rows = field_points.shape[1] // lax.axis_size(SURF)
    place = lax.axis_index

    area = panel_area.reshape(-1, own)
    column, panel_rows = make_start(
        place, forces, panel_plane, area, field_points, lax.axis_size(DEPTH)
    )
    column = exchange(column, DEPTH)
    mine = exchange(make_spread(column, panel_rows, lax.axis_size("s")), "s")
    partner = lax.ppermute(column, "c", SWAP)
    own_tiles, token = make_own(place, wavenumber, column, partner, panel_rows)
    mine, column, partner, token = lax.optimization_barrier((mine, column, partner, token))
    other = lax.ppermute(mine, "c", SWAP)
    keep, give, energy = make_velocity(place, mine, other, response)
    near = exchange(make_pack(keep, lax.ppermute(give, "c", SWAP)), GRID, GATHER)
    energy, column, partner, tile_mine, tile_other, token = lax.optimization_barrier(
        (energy, column, partner, mine, other, token)
    )
    rest_tiles, _ = make_rest(
        place, wavenumber, column, partner, tile_mine, tile_other, token
    )
    partial = make_partial(place, own_tiles, rest_tiles, near)
    level = make_level(exchange(partial, GRID, REDUCE), rows)
    column = exchange(level, DEPTH)
    keep, give, sums = make_finish(place, wavenumber, column, energy, lax.axis_size(LEVEL))
    got = lax.ppermute(give, "c", SWAP)
    sums = make_fold(exchange(sums, LEVEL), lax.axis_size(DEPTH))
    sums = jnp.sum(exchange(sums, DEPTH), axis=0)
    point_total = field_points.shape[1] * lax.axis_size(FIELD)
    panel_total = own * lax.axis_size(SURF + FIELD)
    efficiency = sums[lines:] / point_total / (sums[:lines] / panel_total + 1e-06)
    first = lax.axis_index("c") == 0
    pressure = jnp.concatenate([jnp.where(first, keep, got), jnp.where(first, got, keep)], axis=0)
    pressure = pressure.reshape(lines, rows, 2, cases).transpose(1, 0, 2, 3)
    return (pressure, efficiency)


def solution(mesh):
    grid = Mesh(np.asarray(mesh.devices).reshape(16, 4, 4, 2), SURF + FIELD)
    return jax.shard_map(
        shards,
        mesh=grid,
        in_specs=(
            P(None, None, SURF, None),
            P(None, None, SURF + FIELD, None),
            P(None, SURF),
            P(SURF),
            P(None, FIELD),
            P(),
        ),
        out_specs=(P(FIELD + SURF, None, None, None), P()),
        check_vma=False,
    )
```

```python
import functools
import math

import jax
import jax.numpy as jnp
import numpy as np
from jax import lax
from jax.experimental import pallas as pl
from jax.experimental.pallas import tpu as pltpu
from jax.sharding import Mesh, PartitionSpec as P

SURF = ("s", "zl")
FIELD = ("zh", "c")
DEPTH = ("zh", "zl")
LEVEL = ("s", "c")
SWAP = [(0, 1), (1, 0)]
LANES = 128
STRIP = 32
SIDE = 4
GRID = ("s", "zl", "zh", "c")


def rings(first):
    groups = []
    for zl in range(SIDE):
        for zh in range(SIDE):
            for core in range(2):
                for fixed in range(SIDE):
                    chips = [
                        moving * SIDE + fixed if core == first else fixed * SIDE + moving
                        for moving in range(SIDE)
                    ]
                    groups.append([((chip * SIDE + zl) * SIDE + zh) * 2 + core for chip in chips])
    return groups


GATHER = rings(0)
REDUCE = rings(1)
GROUP = 16
BF16 = jnp.bfloat16
F32 = jnp.float32
INTERPRET = False


def fitted(function, count):
    top = 0.0625
    nodes = 0.5 * top * (1.0 - np.cos(np.pi * (np.arange(count) + 0.5) / count))
    powers = np.vander(nodes, count, increasing=True)
    return [float(value) for value in np.linalg.solve(powers, function(np.sqrt(nodes)))]


SINE = fitted(lambda b: np.sin(2.0 * np.pi * b) / b, 5)
COSINE = fitted(lambda b: np.cos(2.0 * np.pi * b), 5)


def polynomial(coefficients, u):
    total = u * coefficients[-1] + coefficients[-2]
    for value in coefficients[-3::-1]:
        total = total * u + value
    return total


def call(kernel, out, scalars, arrays, name, scratch=(), cost=None, pinned=9):
    single = not isinstance(out, (list, tuple))
    shapes = (out,) if single else tuple(out)
    if INTERPRET:
        results = tuple(jax.ShapeDtypeStruct(s.shape, s.dtype) for s in shapes)
    else:
        results = tuple(pltpu.VMEM(s.shape, s.dtype) for s in shapes)
        arrays = [
            pltpu.with_memory_space_constraint(array, pltpu.VMEM) if index < pinned else array
            for index, array in enumerate(arrays)
        ]
    outs = pl.pallas_call(
        kernel,
        out_shape=results,
        in_specs=[pl.BlockSpec(memory_space=pltpu.SMEM)] * len(scalars)
        + [
            pl.BlockSpec(memory_space=pltpu.VMEM) if index < pinned else pl.BlockSpec()
            for index in range(len(arrays))
        ],
        out_specs=tuple(pl.BlockSpec(memory_space=pltpu.VMEM) for _ in shapes),
        scratch_shapes=list(scratch),
        cost_estimate=cost,
        interpret=INTERPRET,
        name=name,
    )(*scalars, *arrays)
    return outs[0] if single else outs


def cost(flops, moved):
    return pl.CostEstimate(flops=flops, bytes_accessed=moved, transcendentals=0)


def thirds_of(row):
    high = row.astype(BF16).astype(F32)
    middle = (row - high).astype(BF16).astype(F32)
    return [high, middle, row - high - middle]


def start_kernel(place, forces, panel_plane, panel_area, field_points, out, panel_rows):
    zh, core, zl = (place(axis) for axis in ("zh", "c", "zl"))
    x, y = lax.div(place("s"), SIDE), lax.rem(place("s"), SIDE)
    along_y = field_points[:, pl.ds(pl.multiple_of(x * LANES, LANES), LANES)]
    piece = lax.broadcasted_iota(jnp.int32, (3, LANES), 1) // STRIP
    along_x = jnp.zeros((3, LANES), F32)
    for index in range(SIDE):
        shift = lax.rem(index + SIDE - y, SIDE) * STRIP
        moved = pltpu.roll(field_points[:, index * LANES : (index + 1) * LANES], shift, 1)
        along_x = jnp.where(piece == index, moved, along_x)
    point = []
    for block in (
        jnp.where(core == 0, along_y, along_x),
        jnp.where(core == 0, along_x, along_y),
    ):
        row = block[2:3]
        for coordinate in (0, 1):
            row = jnp.where(zl == coordinate, block[coordinate : coordinate + 1], row)
        point += thirds_of(row)
    point = jnp.concatenate(point + [jnp.zeros((2, LANES), F32)], axis=0)
    force = forces[zh, core].astype(F32)
    chunk = jnp.concatenate([force, point], axis=0).astype(BF16)
    for copy in range(out.shape[0]):
        out[copy] = chunk
    for half in range(2):
        field = zh * 2 + lax.rem(core + half, 2)
        lane = pl.multiple_of(field * LANES, LANES)
        rows = thirds_of(panel_plane[0:1, pl.ds(lane, LANES)])
        rows += thirds_of(panel_plane[1:2, pl.ds(lane, LANES)])
        rows += thirds_of(panel_area[pl.ds(field, 1), :])
        rows = jnp.concatenate(rows + [jnp.zeros((GROUP - 9, LANES), F32)], axis=0)
        panel_rows[half] = rows.astype(BF16)


def make_start(place, forces, panel_plane, panel_area, field_points, copies):
    out = (
        jax.ShapeDtypeStruct((copies, GROUP, LANES), BF16),
        jax.ShapeDtypeStruct((2, GROUP, LANES), BF16),
    )
    arrays = [forces, panel_plane, panel_area, field_points]
    return call(functools.partial(start_kernel, place), out, [], arrays, "start", pinned=0)


def spread_kernel(column, panel_rows, out):
    rows = column[:, 0:8, :].astype(F32).reshape(-1, LANES).astype(BF16)
    rows = jnp.concatenate([rows, panel_rows[0]], axis=0)
    for copy in range(out.shape[0]):
        out[copy] = rows


def make_spread(column, panel_rows, copies):
    rows = column.shape[0] * 8 + GROUP
    out = jax.ShapeDtypeStruct((copies, rows, LANES), BF16)
    return call(spread_kernel, out, [], [column, panel_rows], "spread")


def velocity_kernel(place, mine, other, response, keep, give, energy):
    core = place("c")
    lines = response.shape[0]
    depth = response.shape[3] // mine.shape[0]
    for line in range(lines):
        rows = slice(line * depth, (line + 1) * depth)
        a = mine[:, rows, :].reshape(-1, LANES)
        b = other[:, rows, :].reshape(-1, LANES)
        real = jnp.where(core == 0, a, b)
        imag = jnp.where(core == 0, b, a)
        upper = jnp.concatenate([real, imag], axis=1)
        lower = jnp.concatenate([-imag, real], axis=1)
        total = jnp.dot(response[line, 0], upper, preferred_element_type=F32)
        total = total + jnp.dot(response[line, 1], lower, preferred_element_type=F32)
        rounded = total.astype(BF16)
        half, at = divmod(line, lines // 2)

        @pl.when(core == half)
        def _():
            keep[at] = rounded

        @pl.when(core != half)
        def _():
            give[at] = rounded

        wide = rounded.astype(F32)
        squares = jnp.sum(wide * wide, axis=0, keepdims=True)
        energy[line : line + 1, :] = squares[:, :LANES] + squares[:, LANES:]


def make_velocity(place, mine, other, response):
    lines, _, own, channels = response.shape
    half = jax.ShapeDtypeStruct((lines // 2, own, 2 * LANES), BF16)
    out = (half, half, jax.ShapeDtypeStruct((lines, LANES), F32))
    work = cost(8 * lines * own * channels * LANES, 3 << 20)
    kernel = functools.partial(velocity_kernel, place)
    arrays = [mine, other, response]
    return call(kernel, out, [], arrays, "velocity", cost=work, pinned=2)


def pack_kernel(keep, got, out):
    for copy in range(out.shape[0]):
        out[copy, 0] = keep[...]
        out[copy, 1] = got[...]


def make_pack(keep, got):
    out = jax.ShapeDtypeStruct((SIDE, 2) + keep.shape, BF16)
    return call(pack_kernel, out, [], [keep, got], "pack")


def ring_place(place):
    x, y = lax.div(place("s"), SIDE), lax.rem(place("s"), SIDE)
    first = place("c") == 0
    return jnp.where(first, x, y), jnp.where(first, y, x * SIDE), jnp.where(first, SIDE, 1)


def set_points(column, partner, token, px, py, pz):
    for half, (array, base) in enumerate(((column, 8), (partner, 11))):
        for slot in range(4):
            for coordinate, target in enumerate((px, py, pz)):
                part = array[slot * 4 + coordinate].astype(F32)
                row = part[base : base + 1] + part[base + 1 : base + 2] + part[base + 2 : base + 3]
                if coordinate == 2:
                    row = row * row
                block = jnp.broadcast_to(row, (LANES, LANES)).T
                for piece in range(SIDE):
                    start = (piece * 2 + half) * LANES + slot * STRIP
                    target[start : start + STRIP, :] = block[piece * STRIP : (piece + 1) * STRIP, :]
    token[...] = px[0:8, :]


def own_kernel(place, wave, column, partner, panel_rows, out, token, px, py, pz):
    @pl.when(pl.program_id(0) == 0)
    def _():
        set_points(column, partner, token, px, py, pz)

    fill_tiles(place, wave, panel_rows[pl.program_id(0)].astype(F32), out, px, py, pz)


def rest_kernel(place, wave, column, partner, mine, other, before, out, token, px, py, pz):
    last = mine.shape[1] - GROUP
    half, step = pl.program_id(0), pl.program_id(1)

    @pl.when((half == 0) & (step == 0))
    def _():
        set_points(column, partner, token, px, py, pz)

    own, origin, stride = ring_place(place)
    at = origin + stride * jnp.bitwise_xor(own, step + 1)
    thirds = jnp.where(
        half == 0,
        mine[at, last : last + GROUP, :].astype(F32),
        other[at, last : last + GROUP, :].astype(F32),
    )
    fill_tiles(place, wave, thirds, out, px, py, pz)


def fill_tiles(place, wave, thirds, out, px, py, pz):
    lines = out.shape[1]
    across = thirds[0:1] + thirds[1:2] + thirds[2:3]
    along = thirds[3:4] + thirds[4:5] + thirds[5:6]
    area = thirds[6:7] + thirds[7:8] + thirds[8:9]
    turns = [wave[place("c") * lines + line] * (0.5 / math.pi) for line in range(lines)]

    def strip(index, carry):
        rows = pl.ds(pl.multiple_of(index * 64, 64), 64)
        dx = px[rows, :] - across
        dy = py[rows, :] - along
        square = dx * dx + dy * dy + pz[rows, :]
        inverse = lax.rsqrt(square)
        distance = square * inverse
        gain = area * inverse
        opposite = -gain
        for line in range(lines):
            turn = distance * turns[line]
            turn = turn - jnp.round(turn)
            b = 0.25 - jnp.abs(turn)
            u = b * b
            cosine = polynomial(SINE, u) * b
            sine = polynomial(COSINE, u)
            signed = jnp.where(turn < 0.0, opposite, gain)
            out[0, line, rows, 0:LANES] = (signed * sine).astype(BF16)
            out[0, line, rows, LANES : 2 * LANES] = (gain * cosine).astype(BF16)
        return carry

    lax.fori_loop(0, out.shape[2] // 64, strip, 0)


def pinned_to_vmem(array):
    return array if INTERPRET else pltpu.with_memory_space_constraint(array, pltpu.VMEM)


def make_tiles(kernel, wave, columns, arrays, grid, name, after=()):
    points = 8 * LANES
    lines = wave.shape[0] // 2
    vmem = pl.BlockSpec(memory_space=pltpu.VMEM)
    steps = math.prod(grid)
    inner = grid[1] if len(grid) == 2 else 1
    return pl.pallas_call(
        kernel,
        out_shape=(
            jax.ShapeDtypeStruct((steps, lines, points, 2 * LANES), BF16),
            jax.ShapeDtypeStruct((8, LANES), F32),
        ),
        grid=grid,
        in_specs=[pl.BlockSpec(memory_space=pltpu.SMEM)]
        + [pl.BlockSpec(columns[0].shape, lambda *_: (0, 0, 0))] * 2
        + [vmem] * len(arrays)
        + [pl.BlockSpec(memory_space=pl.ANY)] * len(after),
        out_specs=(
            pl.BlockSpec(
                (1, lines, points, 2 * LANES),
                lambda h, i=0: (h * inner + i, 0, 0, 0),
            ),
            pl.BlockSpec((8, LANES), lambda *_: (0, 0)),
        ),
        scratch_shapes=[pltpu.VMEM((points, LANES), F32)] * 3,
        cost_estimate=cost(steps * 1_000_000_000, steps << 20),
        interpret=INTERPRET,
        name=name,
    )(wave, *columns, *[pinned_to_vmem(array) for array in arrays], *after)


def make_own(place, wave, column, partner, panel_rows):
    kernel = functools.partial(own_kernel, place)
    return make_tiles(kernel, wave, [column, partner], [panel_rows], (2,), "own")


def make_rest(place, wave, column, partner, mine, other, before):
    kernel = functools.partial(rest_kernel, place)
    arrays = [mine, other]
    return make_tiles(kernel, wave, [column, partner], arrays, (2, 3), "rest", (before,))


def partial_kernel(place, *refs):
    tiles, near, out = refs[:8], refs[8], refs[-1]
    line = pl.program_id(0)
    own, _, _ = ring_place(place)
    total = None
    for half in range(2):
        for step in range(SIDE):
            upper = near[jnp.bitwise_xor(own, step), half, line]
            lower = jnp.concatenate([-upper[:, LANES:], upper[:, :LANES]], axis=1)
            stacked = jnp.concatenate([upper, lower], axis=0)
            tile = tiles[half * SIDE + step][0, 0]
            term = jnp.dot(tile, stacked, preferred_element_type=F32)
            total = term if total is None else total + term
    parts, _, share, columns = out.shape
    out[:, 0] = total.astype(BF16).reshape(parts, share, columns)


def make_partial(place, own, rest, near):
    _, lines, points, depth = own.shape
    columns = near.shape[-1]
    step_rows = points // 2
    share = points // SIDE
    specs = []
    for half in range(2):
        for step in range(SIDE):
            at = half if step == 0 else half * 3 + step - 1
            specs.append(
                pl.BlockSpec((1, 1, step_rows, depth), lambda l, i, at=at: (at, l, i, 0))
            )
    return pl.pallas_call(
        functools.partial(partial_kernel, place),
        out_shape=jax.ShapeDtypeStruct((SIDE, lines, share, columns), BF16),
        grid=(lines, 2),
        in_specs=specs + [pl.BlockSpec(memory_space=pltpu.VMEM)],
        out_specs=pl.BlockSpec((2, 1, share, columns), lambda l, i: (i, l, 0, 0)),
        cost_estimate=cost(16 * lines * points * depth * columns, 10 << 20),
        interpret=INTERPRET,
        name="partial",
    )(*(([own] + [rest] * 3) * 2), pinned_to_vmem(near))


def level_kernel(rows, beside, out):
    levels = []
    for line in range(beside.shape[1]):
        total = beside[0, line].astype(F32)
        for source in range(1, beside.shape[0]):
            total = total + beside[source, line].astype(F32)
        share = total.shape[0] // 2
        for half in range(2):
            part = total[half * share : (half + 1) * share]
            levels.append(part.reshape(-1, rows, total.shape[1]))
    out[...] = jnp.concatenate(levels, axis=1).astype(BF16)


def make_level(beside, rows):
    _, lines, share, columns = beside.shape
    out = jax.ShapeDtypeStruct((share // (2 * rows), lines * 2 * rows, columns), BF16)
    return call(functools.partial(level_kernel, rows), out, [], [beside], "level")


def finish_kernel(place, wave, column, energy, keep, give, sums):
    lines = energy.shape[0]
    core = place("c")
    total = column[0].astype(F32)
    for source in range(1, column.shape[0]):
        total = total + column[source].astype(F32)
    half = lines // 2
    share = total.shape[0] // half
    rows = share // 2
    parts = [
        total[line * share : (line + 1) * share] * (wave[core * half + line] * (0.5 / math.pi))
        for line in range(half)
    ]
    rounded = jnp.concatenate(parts, axis=0).astype(BF16)
    wide = rounded.astype(F32)
    for line in range(half):
        start = line * share
        keep[line * rows : (line + 1) * rows, :] = wide[start : start + rows].astype(BF16)
        give[line * rows : (line + 1) * rows, :] = wide[start + rows : start + share].astype(BF16)
    wide = wide * wide
    both = wide[:, :LANES] + wide[:, LANES:]
    power = [
        jnp.sum(both[line * share : (line + 1) * share], axis=0, keepdims=True)
        for line in range(half)
    ]
    nothing = jnp.zeros_like(power[0])
    power = [jnp.where(core == line // half, power[line % half], nothing) for line in range(lines)]
    table = jnp.concatenate([energy[...]] + power, axis=0)
    for copy in range(sums.shape[0]):
        sums[copy] = table


def make_finish(place, wave, column, energy, copies):
    lines, cases = energy.shape
    _, rows, columns = column.shape
    half = jax.ShapeDtypeStruct((rows // 2, columns), BF16)
    out = (half, half, jax.ShapeDtypeStruct((copies, 2 * lines, cases), F32))
    kernel = functools.partial(finish_kernel, place)
    return call(kernel, out, [wave], [column, energy], "finish")


def fold_kernel(table, out):
    total = table[0]
    for source in range(1, table.shape[0]):
        total = total + table[source]
    for copy in range(out.shape[0]):
        out[copy] = total


def make_fold(table, copies):
    out = jax.ShapeDtypeStruct((copies,) + table.shape[1:], F32)
    return call(fold_kernel, out, [], [table], "fold")


def exchange(array, axes, groups=None):
    return lax.all_to_all(array, axes, 0, 0, tiled=True, axis_index_groups=groups)


def shards(forces, response, panel_plane, panel_area, field_points, wavenumber):
    lines, _, channels, cases = forces.shape
    own = response.shape[2]
    rows = field_points.shape[1] // lax.axis_size(SURF)
    place = lax.axis_index

    area = panel_area.reshape(-1, own)
    column, panel_rows = make_start(
        place, forces, panel_plane, area, field_points, lax.axis_size(DEPTH)
    )
    column = exchange(column, DEPTH)
    mine = exchange(make_spread(column, panel_rows, lax.axis_size("s")), "s")
    partner = lax.ppermute(column, "c", SWAP)
    own_tiles, token = make_own(place, wavenumber, column, partner, panel_rows)
    mine, column, partner, token = lax.optimization_barrier((mine, column, partner, token))
    other = lax.ppermute(mine, "c", SWAP)
    keep, give, energy = make_velocity(place, mine, other, response)
    near = exchange(make_pack(keep, lax.ppermute(give, "c", SWAP)), GRID, GATHER)
    energy, column, partner, tile_mine, tile_other, token = lax.optimization_barrier(
        (energy, column, partner, mine, other, token)
    )
    rest_tiles, _ = make_rest(
        place, wavenumber, column, partner, tile_mine, tile_other, token
    )
    partial = make_partial(place, own_tiles, rest_tiles, near)
    level = make_level(exchange(partial, GRID, REDUCE), rows)
    column = exchange(level, DEPTH)
    keep, give, sums = make_finish(place, wavenumber, column, energy, lax.axis_size(LEVEL))
    got = lax.ppermute(give, "c", SWAP)
    sums = make_fold(exchange(sums, LEVEL), lax.axis_size(DEPTH))
    sums = jnp.sum(exchange(sums, DEPTH), axis=0)
    point_total = field_points.shape[1] * lax.axis_size(FIELD)
    panel_total = own * lax.axis_size(SURF + FIELD)
    efficiency = sums[lines:] / point_total / (sums[:lines] / panel_total + 1e-06)
    first = lax.axis_index("c") == 0
    pressure = jnp.concatenate([jnp.where(first, keep, got), jnp.where(first, got, keep)], axis=0)
    pressure = pressure.reshape(lines, rows, 2, cases).transpose(1, 0, 2, 3)
    return (pressure, efficiency)


def solution(mesh):
    grid = Mesh(np.asarray(mesh.devices).reshape(16, 4, 4, 2), SURF + FIELD)
    return jax.shard_map(
        shards,
        mesh=grid,
        in_specs=(
            P(None, None, SURF, None),
            P(None, None, SURF + FIELD, None),
            P(None, SURF),
            P(SURF),
            P(None, FIELD),
            P(),
        ),
        out_specs=(P(FIELD + SURF, None, None, None), P()),
        check_vma=False,
    )
```
